256 devices in a mesh: dp: 8 (over x, core), group: 32 (over z, y).
Axes of the slice: x: 4, y: 4, z: 8, core: 2. Of those that a mesh axis runs over, the one named last changes fastest.
Arguments:
- embeds: bfloat16 [65536, 1024], P(('dp', 'group')), may hold values from -6 to 6
- row_ids: int32 [65536], P(('dp', 'group')), may hold values from 0 to 63
- neighbors: int32 [256, 3], P('dp'), may hold values from 0 to 31, as said below
- w_first: bfloat16 [1024, 4096], P(None, 'dp'), may hold values from -0.1875 to 0.1875
- w_second: bfloat16 [4096, 1024], P('dp'), may hold values from -0.09375 to 0.09375
Outputs:
- grad_first: float32 [1024, 4096], P('group', 'dp')
- grad_second: float32 [4096, 1024], P('dp', 'group')
- grad_unit: float32 [65536, 1024], P(('dp', 'group'))
The draws below stay inside these ranges and needn't reach their ends.
Inputs may be any that keep to these rules, and one draw needn't show every extreme that they name: `neighbors`: within a row the 3 entries differ from one another and from the row's own index b % 32.
All inputs are finite; a program needn't handle non-finite values.
Results may differ from the reference program's by a relative error of at most 0.013.
Values may be sent and summed in bfloat16 or wider, within the bound.
No kernel may reach another device: no remote copies, remote signals or barrier semaphores. Data moves between devices by JAX's collectives and lax.ppermute only.
A program may use at most 64 MiB of HBM per device.

```python
import jax
import jax.numpy as jnp
from jax import lax

E = 1024
H = 4096
P_SIZE = 1024
BLOCK = 256
K = 3
CLASSES = 64
OWNERS = 32
N_BLOCKS = 256
ROWS = 65536
N_DP = 8


CLASS_SHARE = 0.6


LATENT_SHARE = 0.8


def shared_trace_ids(key):
    return jax.random.randint(jax.random.fold_in(key, 11), (ROWS,), 0, CLASSES).astype(jnp.int32)


def draw_row_ids(key, part):
    return shared_trace_ids(key)


def draw_embeds(key, part):
    trace_ids = shared_trace_ids(key)
    streams = jax.random.split(jax.random.fold_in(key, 23), 4)
    latent = jax.random.normal(streams[0], (CLASSES, 4), jnp.float32)
    squares = latent * latent
    length = squares[:, 0] + squares[:, 1] + squares[:, 2] + squares[:, 3]
    latent = latent * lax.rsqrt(jnp.maximum(length, 0.0001))[:, None]
    basis = jax.random.normal(streams[1], (4, E), jnp.float32)
    mixed = latent[:, 0:1] * basis[0][None, :] + latent[:, 1:2] * basis[1][None, :] + latent[:, 2:3] * basis[2][None, :] + latent[:, 3:4] * basis[3][None, :]
    apart = jax.random.normal(streams[2], (CLASSES, E), jnp.float32)
    classes = jnp.sqrt(LATENT_SHARE) * mixed + jnp.sqrt(1.0 - LATENT_SHARE) * apart
    noise = jax.random.normal(streams[3], (ROWS, E), jnp.float32)
    class_rows = jnp.take(classes, trace_ids, axis=0)
    values = jnp.sqrt(1.0 - CLASS_SHARE) * noise + jnp.sqrt(CLASS_SHARE) * class_rows
    return jnp.clip(values, -6.0, 6.0).astype(jnp.bfloat16)


def draw_neighbors(key, part):
    key_pop, key_noise = jax.random.split(jax.random.fold_in(key, 17))
    slices = N_BLOCKS // OWNERS
    popular = jax.random.randint(key_pop, (slices, 1, OWNERS), 0, 4)
    noise = jax.random.randint(key_noise, (slices, OWNERS, OWNERS), 0, 65536)
    target = jnp.arange(OWNERS, dtype=jnp.int32)
    priority = (popular * 65536 + noise) * OWNERS + target[None, None, :]
    own = target[:, None] == target[None, :]
    priority = jnp.where(own[None], -1, priority)
    _, chosen = lax.top_k(priority, K)
    return chosen.reshape(N_BLOCKS, K).astype(jnp.int32)


def shard_levels(stream_key, extent, cuts, least, top_value):
    gain, own = 1.0, jax.random.fold_in(stream_key, 6)
    for dim, shards_of in cuts:
        steps = jnp.exp(jax.random.uniform(jax.random.fold_in(own, dim), (shards_of,), jnp.float32, least / len(cuts), top_value / len(cuts)))
        gain = gain * jnp.repeat(steps, extent[dim] // shards_of).reshape([-1 if axis == dim else 1 for axis in range(len(extent))])
    return gain


def bell_draw(key, extent, width, bound, cuts=(), kind=jnp.bfloat16):
    array = jax.random.normal(key, extent, jnp.float32) * width
    if len(cuts) > 0:
        array = shard_levels(key, extent, cuts, -0.22, 0.18) * array
    return jnp.clip(array, min=-bound, max=bound).astype(kind)


def setup_inputs(seed: int = 0) -> dict:
    seeds = jax.random.split(jax.random.key(seed), 6)
    return {
        "embeds": draw_embeds(jax.random.fold_in(seeds[5], 71), 0),
        "row_ids": draw_row_ids(jax.random.fold_in(seeds[5], 71), 0),
        "neighbors": draw_neighbors(jax.random.fold_in(seeds[5], 71), 0),
        "w_first": bell_draw(seeds[3], (E, H), E ** -0.5, 0.1875, ((1, 8),)),
        "w_second": bell_draw(seeds[4], (H, P_SIZE), H ** -0.5, 0.09375, ((0, 8),)),
    }


EPS = 1e-06
TEMP = 10.0
SHIFT = -5.0

def gelu_fwd(value):
    return jax.nn.gelu(value, approximate=True)

def gelu_back(pre, grad):
    _, back = jax.vjp(gelu_fwd, pre)
    return back(grad)[0]

def block_terms(own, own_ids, cand, cand_ids):
    logits = TEMP / P_SIZE * jnp.einsum('rp,kcp->krc', own, cand) + SHIFT
    sign = jnp.where(own_ids[None, :, None] == cand_ids[:, None, :], 1.0, -1.0).astype(jnp.float32)
    weight = (-sign * jax.nn.sigmoid(-sign * logits) * (TEMP / P_SIZE)).astype(jnp.bfloat16)
    weight = lax.optimization_barrier(weight).astype(jnp.float32)
    grad_own = jnp.einsum('krc,kcp->rp', weight, cand)
    grad_cand = jnp.einsum('krc,rp->kcp', weight, own)
    return (grad_own, grad_cand)

def slice_terms(inputs):
    units, ids, lists = inputs

    def one_block(inner):
        own, own_ids, listed = inner
        cand = jnp.concatenate([own[None], jnp.take(units, listed, axis=0)], 0).astype(jnp.float32)
        cand_ids = jnp.concatenate([own_ids[None], jnp.take(ids, listed, axis=0)], 0)
        return block_terms(own.astype(jnp.float32), own_ids, cand, cand_ids)
    grad_own, grad_cand = lax.map(one_block, (units, ids, lists))
    returned = jnp.zeros((OWNERS, BLOCK, P_SIZE), jnp.float32).at[lists.reshape(-1)].add(grad_cand[:, 1:].reshape(-1, BLOCK, P_SIZE))
    return grad_own + grad_cand[:, 0] + returned

def reference(embeds, row_ids, neighbors, w_first, w_second):
    share = H // N_DP
    proj = jnp.zeros((ROWS, P_SIZE), jnp.float32)
    for index in range(N_DP):
        pre = jnp.dot(embeds, w_first[:, index * share:(index + 1) * share], preferred_element_type=jnp.float32)
        hidden = gelu_fwd(pre).astype(jnp.bfloat16)
        part = jnp.dot(hidden, w_second[index * share:(index + 1) * share], preferred_element_type=jnp.float32)
        part = lax.optimization_barrier(part.astype(jnp.bfloat16)).astype(jnp.float32)
        proj = proj + part
    inv = lax.rsqrt(lax.optimization_barrier(jnp.mean(proj * proj, axis=-1, keepdims=True)) + EPS)
    unit = proj * inv
    unit_b = unit.astype(jnp.bfloat16)
    grad_unit = lax.map(slice_terms, (unit_b.reshape(N_DP, OWNERS, BLOCK, P_SIZE), row_ids.reshape(N_DP, OWNERS, BLOCK), neighbors.reshape(N_DP, OWNERS, K)))
    grad_unit = grad_unit.reshape(ROWS, P_SIZE)
    grad_proj = (inv * (grad_unit - unit * lax.optimization_barrier(jnp.mean(unit * grad_unit, axis=-1, keepdims=True)))).astype(jnp.bfloat16)
    firsts = []
    seconds = []
    for index in range(N_DP):
        w_part = w_second[index * share:(index + 1) * share]
        pre = jnp.dot(embeds, w_first[:, index * share:(index + 1) * share], preferred_element_type=jnp.float32)
        hidden = gelu_fwd(pre).astype(jnp.bfloat16)
        seconds.append(jnp.dot(hidden.T, grad_proj, preferred_element_type=jnp.float32))
        grad_hidden = jnp.dot(grad_proj, w_part.T, preferred_element_type=jnp.float32)
        grad_pre = gelu_back(pre, grad_hidden).astype(jnp.bfloat16)
        firsts.append(jnp.dot(embeds.T, grad_pre, preferred_element_type=jnp.float32))
    return (jnp.concatenate(firsts, 1), jnp.concatenate(seconds, 0), grad_unit)
```

```python
import jax
import jax.numpy as jnp
from jax import lax
from jax.experimental import pallas as pl
from jax.experimental.pallas import tpu as pltpu
from jax.sharding import Mesh, PartitionSpec as P

EPS = 1e-06
TEMP = 10.0
SHIFT = -5.0
F32, BF16 = jnp.float32, jnp.bfloat16


def gelu_fwd(value):
    return jax.nn.gelu(value, approximate=True)


def gelu_back(pre, grad):
    _, back = jax.vjp(gelu_fwd, pre)
    return back(grad)[0]


def shift(value, axis, step):
    n = lax.axis_size(axis)
    return lax.ppermute(value, axis, [(i, (i + step) % n) for i in range(n)])


def swap_core(value):
    return lax.ppermute(value, "core", [(0, 1), (1, 0)])


def offsets(n):
    out = [0]
    for t in range(1, n // 2):
        out += [-t, t]
    return out + [n // 2]


def slot_of(offset, n):
    table = [0] * n
    for place, t in enumerate(offsets(n)):
        table[t % n] = place
    offset = lax.rem(offset + 2 * n, n)
    return sum(jnp.where(offset == t, table[t], 0) for t in range(1, n))


def ring_gather(block, axis):
    half, rows = lax.axis_size(axis) // 2, block.shape[0] // 2
    out, up, down = [block], block, block
    for _ in range(1, half):
        up, down = shift(up, axis, 1), shift(down, axis, -1)
        out += [up, down]
    return out + [shift(up[:rows], axis, 1), shift(down[rows:], axis, -1)]


def ring_scatter(part, axis, dtype):
    half = lax.axis_size(axis) // 2
    far = part(half)
    rows = far.shape[0] // 2
    up = shift(far[:rows].astype(dtype), axis, 1).astype(F32)
    down = shift(far[rows:].astype(dtype), axis, -1).astype(F32)
    for t in range(half - 1, 0, -1):
        a, b = part(t), part(-t)
        if t == half - 1:
            a = jnp.concatenate([a[:rows] + up, a[rows:]], 0)
            b = jnp.concatenate([b[:rows], b[rows:] + down], 0)
        else:
            a, b = a + up, b + down
        up = shift(a.astype(dtype), axis, 1).astype(F32)
        down = shift(b.astype(dtype), axis, -1).astype(F32)
    return part(0) + up + down


def gather_dp(block):
    own, up, down, far_up, far_down = ring_gather(block, "x")
    near, far = jnp.concatenate([up, down], 0), jnp.concatenate([far_up, far_down], 0)
    pieces = [own, near, far]
    return jnp.concatenate(pieces + [swap_core(p) for p in pieces], 0)


def pair_kernel(n_z, n_y, at_z, at_y, blocks, mult, count, own_ref, own_ids_ref, ids_ref,
                unit_ref, inv_ref, *refs):
    n_a, n_b = n_z + 1, n_y + 1
    pieces_a, pieces_b = refs[:n_a], refs[n_a:n_a + n_b]
    grad_unit_ref, grad_proj_ref, cand_ref, sems = refs[n_a + n_b:]
    width, half = own_ref.shape[1], own_ref.shape[0] // 2

    def start(i, slot):
        for pieces, outer, inner, n_in, part in (
            (pieces_a, at_z[i], at_y[i], n_y, 0),
            (pieces_b, at_y[i], at_z[i], n_z, 1),
        ):
            far = len(pieces) - 2
            source = jnp.where((outer == far) & (inner >= n_in // 2), far + 1, outer)
            row = jnp.where(source == far + 1, inner - n_in // 2, inner) * half
            for k, piece in enumerate(pieces):

                @pl.when(source == k)
                def _():
                    pltpu.make_async_copy(
                        piece.at[pl.ds(pl.multiple_of(row, half), half)],
                        cand_ref.at[slot, pl.ds(part * half, half)],
                        sems.at[slot, part],
                    ).start()

    def wait(slot):
        for part in range(2):
            pltpu.make_async_copy(
                pieces_a[0].at[pl.ds(0, half)],
                cand_ref.at[slot, pl.ds(part * half, half)],
                sems.at[slot, part],
            ).wait()

    def body(i, carry):
        slot = lax.rem(i, 2)

        @pl.when(i + 1 < count[0])
        def _():
            start(i + 1, 1 - slot)

        wait(slot)
        cand = cand_ref[slot]
        logits = lax.dot_general(
            own_ref[...], cand, (((1,), (1,)), ((), ())), preferred_element_type=F32
        ) * (TEMP / width) + SHIFT
        same = own_ids_ref[...] == ids_ref[blocks[i]]
        sign = jnp.where(same, 1.0, -1.0).astype(F32)
        scale = mult[i].astype(F32) * (-TEMP / width)
        weight = (sign * scale / (1.0 + jnp.exp(sign * logits))).astype(BF16)
        grad_unit_ref[...] += jnp.dot(weight, cand, preferred_element_type=F32)
        return carry

    start(0, 0)
    grad_unit_ref[...] = jnp.zeros_like(grad_unit_ref)
    lax.fori_loop(0, count[0], body, 0)
    total, unit = grad_unit_ref[...], unit_ref[...]
    mean = jnp.mean(unit * total, axis=-1, keepdims=True)
    grad_proj_ref[...] = (inv_ref[...] * (total - unit * mean)).astype(BF16)


def pair_grads(lists, own, own_ids, ids, pieces_a, pieces_b, unit, inv):
    rows, width = own.shape
    n_z, n_y = len(pieces_a) - 1, len(pieces_b) - 1
    vmem = pl.BlockSpec(memory_space=pltpu.VMEM)
    smem = pl.BlockSpec(memory_space=pltpu.SMEM)
    return pl.pallas_call(
        lambda *refs: pair_kernel(n_z, n_y, *refs),
        in_specs=[smem] * 5 + [vmem] * 5
        + [pl.BlockSpec(memory_space=pl.ANY)] * (n_z + n_y + 2),
        out_specs=[vmem] * 2,
        out_shape=[
            jax.ShapeDtypeStruct((rows, width), F32),
            jax.ShapeDtypeStruct((rows, width), BF16),
        ],
        scratch_shapes=[
            pltpu.VMEM((2, rows, width), BF16),
            pltpu.SemaphoreType.DMA((2, 2)),
        ],
        compiler_params=pltpu.CompilerParams(vmem_limit_bytes=20 << 20),
    )(*lists, own, own_ids, ids, unit, inv, *pieces_a, *pieces_b)


def partner_lists(neighbors, n_z, n_y):
    owners = n_z * n_y
    z, y = lax.axis_index("z"), lax.axis_index("y")
    me = z * n_y + y
    block = jnp.arange(owners, dtype=jnp.int32)
    listed = neighbors[None, :, :] == block[:, None, None]
    mine = block == me
    out = jnp.sum(jnp.where(mine[None, :, None], listed, False), axis=(1, 2))
    into = jnp.sum(neighbors == me, axis=1)
    mult = (out + into + 2 * mine).astype(jnp.int32)
    used = mult > 0
    place = jnp.sum(used[None, :] & (block[None, :] < block[:, None]), axis=1)
    pick = used[None, :] & (place[None, :] == block[:, None])
    count = jnp.sum(used).astype(jnp.int32)
    pick = jnp.where((block < count)[:, None], pick, used[None, :] & (place[None, :] == count - 1))
    blocks = jnp.sum(jnp.where(pick, block[None, :], 0), axis=1).astype(jnp.int32)
    mult = jnp.sum(jnp.where(pick, mult[None, :], 0), axis=1).astype(jnp.int32)
    at_z = slot_of(blocks // n_y - z, n_z)
    at_y = slot_of(lax.rem(blocks, n_y) - y, n_y)
    lists = (at_z, at_y, blocks, mult)
    return tuple(v.astype(jnp.int32) for v in lists) + (count[None],)


def per_device(embeds, row_ids, neighbors, w_first, w_second):
    n_z, n_y = lax.axis_size("z"), lax.axis_size("y")
    owners = n_z * n_y
    z, y = lax.axis_index("z"), lax.axis_index("y")
    block, width = embeds.shape[0], w_second.shape[1]
    share = w_first.shape[1]
    half = block // 2

    ids = lax.all_gather(row_ids, ("z", "y"), axis=0, tiled=True).reshape(owners, 1, block)
    lists = partner_lists(neighbors, n_z, n_y)

    rows = gather_dp(embeds)
    pre = jnp.dot(rows, w_first, preferred_element_type=F32)
    hidden = gelu_fwd(pre).astype(BF16)
    part = jnp.dot(hidden, w_second, preferred_element_type=F32).astype(BF16)
    n_x = lax.axis_size("x")
    part = part.reshape(2, n_x, block, width)
    pair = part[0].astype(F32) + swap_core(part[1]).astype(F32)
    place = {t: i for i, t in enumerate(offsets(n_x))}
    proj = ring_scatter(lambda t: pair[place[t]], "x", BF16)

    inv = lax.rsqrt(jnp.mean(proj * proj, axis=-1, keepdims=True) + EPS)
    unit = proj * inv
    unit_b = unit.astype(BF16)

    over_y = jnp.concatenate(ring_gather(unit_b[:half], "y"), 0)
    over_z = jnp.concatenate(ring_gather(unit_b[half:], "z"), 0)
    units_a = ring_gather(over_y, "z")
    units_b = ring_gather(over_z, "y")
    grad_unit, grad_proj = pair_grads(
        lists, unit_b, row_ids[:, None], ids, units_a, units_b, unit, inv
    )

    grad_all = gather_dp(grad_proj)
    rows_in = (((0,), (0,)), ((), ()))
    second = lax.dot_general(grad_all, hidden, rows_in, preferred_element_type=F32)
    grad_hidden = lax.dot_general(
        grad_all, w_second, (((1,), (1,)), ((), ())), preferred_element_type=F32
    )
    grad_pre = gelu_back(pre, grad_hidden).astype(BF16)
    first = lax.dot_general(rows, grad_pre, rows_in, preferred_element_type=F32)

    second = lax.psum_scatter(second, "z", scatter_dimension=0, tiled=True)
    second = lax.psum_scatter(second, "y", scatter_dimension=0, tiled=True)

    first = first.reshape(n_z, n_y, -1, share)
    first = ring_scatter(
        lambda t: lax.dynamic_index_in_dim(first, lax.rem(y + t + n_y, n_y), 1, False), "y", F32
    )
    by_z = first
    first = ring_scatter(
        lambda t: lax.dynamic_index_in_dim(by_z, lax.rem(z + t + n_z, n_z), 0, False), "z", F32
    )
    return (first, second.T, grad_unit)


def solution(mesh):
    split = Mesh(mesh.devices.reshape(4, 2, 8, 4), ("x", "core", "z", "y"))
    dp, group = ("x", "core"), ("z", "y")
    in_specs = (P(dp + group, None), P(dp + group), P(dp, None), P(None, dp), P(dp, None))
    out_specs = (P(group, dp), P(dp, group), P(dp + group, None))
    return jax.shard_map(
        per_device, mesh=split, in_specs=in_specs, out_specs=out_specs, check_vma=False
    )
```

```python
import jax
import jax.numpy as jnp
from jax import lax
from jax.experimental import pallas as pl
from jax.experimental.pallas import tpu as pltpu
from jax.sharding import Mesh, PartitionSpec as P

EPS = 1e-06
TEMP = 10.0
SHIFT = -5.0
F32, BF16 = jnp.float32, jnp.bfloat16


def gelu_fwd(value):
    return jax.nn.gelu(value, approximate=True)


def gelu_back(pre, grad):
    _, back = jax.vjp(gelu_fwd, pre)
    return back(grad)[0]


def shift(value, axis, step):
    n = lax.axis_size(axis)
    return lax.ppermute(value, axis, [(i, (i + step) % n) for i in range(n)])


def swap_core(value):
    return lax.ppermute(value, "core", [(0, 1), (1, 0)])


def offsets(n):
    out = [0]
    for t in range(1, n // 2):
        out += [-t, t]
    return out + [n // 2]


def slot_of(offset, n):
    table = [0] * n
    for place, t in enumerate(offsets(n)):
        table[t % n] = place
    offset = lax.rem(offset + 2 * n, n)
    return sum(jnp.where(offset == t, table[t], 0) for t in range(1, n))


def ring_gather(block, axis):
    half, rows = lax.axis_size(axis) // 2, block.shape[0] // 2
    out, up, down = [block], block, block
    for _ in range(1, half):
        up, down = shift(up, axis, 1), shift(down, axis, -1)
        out += [up, down]
    return out + [shift(up[:rows], axis, 1), shift(down[rows:], axis, -1)]


def ring_scatter(part, axis, dtype):
    half = lax.axis_size(axis) // 2
    far = part(half)
    rows = far.shape[0] // 2
    up = shift(far[:rows].astype(dtype), axis, 1).astype(F32)
    down = shift(far[rows:].astype(dtype), axis, -1).astype(F32)
    for t in range(half - 1, 0, -1):
        a, b = part(t), part(-t)
        if t == half - 1:
            a = jnp.concatenate([a[:rows] + up, a[rows:]], 0)
            b = jnp.concatenate([b[:rows], b[rows:] + down], 0)
        else:
            a, b = a + up, b + down
        up = shift(a.astype(dtype), axis, 1).astype(F32)
        down = shift(b.astype(dtype), axis, -1).astype(F32)
    return part(0) + up + down


def gather_dp(block):
    own, up, down, far_up, far_down = ring_gather(block, "x")
    near, far = jnp.concatenate([up, down], 0), jnp.concatenate([far_up, far_down], 0)
    pieces = [own, near, far]
    return jnp.concatenate(pieces + [swap_core(p) for p in pieces], 0)


def pair_kernel(n_z, n_y, at_z, at_y, blocks, mult, count, own_ref, own_ids_ref, ids_ref,
                unit_ref, inv_ref, *refs):
    n_a, n_b = n_z + 1, n_y + 1
    pieces_a, pieces_b = refs[:n_a], refs[n_a:n_a + n_b]
    grad_unit_ref, grad_proj_ref, cand_ref, sems = refs[n_a + n_b:]
    width = own_ref.shape[1]
    rows_a = pieces_a[0].shape[0] // n_y
    spans = ((0, rows_a), (rows_a, own_ref.shape[0] - rows_a))

    def start(i, slot):
        for pieces, outer, inner, n_in, part in (
            (pieces_a, at_z[i], at_y[i], n_y, 0),
            (pieces_b, at_y[i], at_z[i], n_z, 1),
        ):
            far = len(pieces) - 2
            source = jnp.where((outer == far) & (inner >= n_in // 2), far + 1, outer)
            first, rows = spans[part]
            row = jnp.where(source == far + 1, inner - n_in // 2, inner) * rows
            for k, piece in enumerate(pieces):

                @pl.when(source == k)
                def _():
                    pltpu.make_async_copy(
                        piece.at[pl.ds(pl.multiple_of(row, 16), rows)],
                        cand_ref.at[slot, pl.ds(first, rows)],
                        sems.at[slot, part],
                    ).start()

    def wait(slot):
        for part, (first, rows) in enumerate(spans):
            pltpu.make_async_copy(
                pieces_b[0].at[pl.ds(0, rows)],
                cand_ref.at[slot, pl.ds(first, rows)],
                sems.at[slot, part],
            ).wait()

    def body(i, carry):
        slot = lax.rem(i, 2)

        @pl.when(i + 1 < count[0])
        def _():
            start(i + 1, 1 - slot)

        wait(slot)
        cand = cand_ref[slot]
        logits = lax.dot_general(
            own_ref[...], cand, (((1,), (1,)), ((), ())), preferred_element_type=F32
        ) * (TEMP / width) + SHIFT
        same = own_ids_ref[...] == ids_ref[blocks[i]]
        sign = jnp.where(same, 1.0, -1.0).astype(F32)
        scale = mult[i].astype(F32) * (-TEMP / width)
        weight = (sign * scale / (1.0 + jnp.exp(sign * logits))).astype(BF16)
        grad_unit_ref[...] += jnp.dot(weight, cand, preferred_element_type=F32)
        return carry

    start(0, 0)
    grad_unit_ref[...] = jnp.zeros_like(grad_unit_ref)
    lax.fori_loop(0, count[0], body, 0)
    total, unit = grad_unit_ref[...], unit_ref[...]
    mean = jnp.mean(unit * total, axis=-1, keepdims=True)
    grad_proj_ref[...] = (inv_ref[...] * (total - unit * mean)).astype(BF16)


def pair_grads(lists, own, own_ids, ids, pieces_a, pieces_b, unit, inv):
    rows, width = own.shape
    n_z, n_y = len(pieces_a) - 1, len(pieces_b) - 1
    vmem = pl.BlockSpec(memory_space=pltpu.VMEM)
    smem = pl.BlockSpec(memory_space=pltpu.SMEM)
    return pl.pallas_call(
        lambda *refs: pair_kernel(n_z, n_y, *refs),
        in_specs=[smem] * 5 + [vmem] * 5
        + [pl.BlockSpec(memory_space=pl.ANY)] * (n_z + n_y + 2),
        out_specs=[vmem] * 2,
        out_shape=[
            jax.ShapeDtypeStruct((rows, width), F32),
            jax.ShapeDtypeStruct((rows, width), BF16),
        ],
        scratch_shapes=[
            pltpu.VMEM((2, rows, width), BF16),
            pltpu.SemaphoreType.DMA((2, 2)),
        ],
        compiler_params=pltpu.CompilerParams(vmem_limit_bytes=20 << 20),
    )(*lists, own, own_ids, ids, unit, inv, *pieces_a, *pieces_b)


def partner_lists(neighbors, n_z, n_y):
    owners = n_z * n_y
    z, y = lax.axis_index("z"), lax.axis_index("y")
    me = z * n_y + y
    block = jnp.arange(owners, dtype=jnp.int32)
    listed = neighbors[None, :, :] == block[:, None, None]
    mine = block == me
    out = jnp.sum(jnp.where(mine[None, :, None], listed, False), axis=(1, 2))
    into = jnp.sum(neighbors == me, axis=1)
    mult = (out + into + 2 * mine).astype(jnp.int32)
    used = mult > 0
    place = jnp.sum(used[None, :] & (block[None, :] < block[:, None]), axis=1)
    pick = used[None, :] & (place[None, :] == block[:, None])
    count = jnp.sum(used).astype(jnp.int32)
    pick = jnp.where((block < count)[:, None], pick, used[None, :] & (place[None, :] == count - 1))
    blocks = jnp.sum(jnp.where(pick, block[None, :], 0), axis=1).astype(jnp.int32)
    mult = jnp.sum(jnp.where(pick, mult[None, :], 0), axis=1).astype(jnp.int32)
    at_z = slot_of(blocks // n_y - z, n_z)
    at_y = slot_of(lax.rem(blocks, n_y) - y, n_y)
    lists = (at_z, at_y, blocks, mult)
    return tuple(v.astype(jnp.int32) for v in lists) + (count[None],)


def per_device(embeds, row_ids, neighbors, w_first, w_second):
    n_z, n_y = lax.axis_size("z"), lax.axis_size("y")
    owners = n_z * n_y
    z, y = lax.axis_index("z"), lax.axis_index("y")
    block, width = embeds.shape[0], w_second.shape[1]
    share = w_first.shape[1]
    part_a = block * 7 // 16

    ids, embeds = lax.optimization_barrier((jnp.broadcast_to(row_ids[None], (32, block)), embeds))
    ids = lax.optimization_barrier(lax.all_gather(ids, ("z", "y"), axis=0))[:, :1]
    lists = partner_lists(neighbors, n_z, n_y)

    rows = gather_dp(embeds)
    pre = jnp.dot(rows, w_first, preferred_element_type=F32)
    hidden = lax.optimization_barrier(gelu_fwd(pre).astype(BF16))
    slope = lax.optimization_barrier(gelu_back(pre, jnp.ones_like(pre)))
    part = jnp.dot(hidden, w_second, preferred_element_type=F32).astype(BF16)
    n_x = lax.axis_size("x")
    part = part.reshape(2, n_x, block, width)
    pair = part[0].astype(F32) + swap_core(part[1]).astype(F32)
    place = {t: i for i, t in enumerate(offsets(n_x))}
    proj = ring_scatter(lambda t: pair[place[t]], "x", BF16)

    inv = lax.rsqrt(jnp.mean(proj * proj, axis=-1, keepdims=True) + EPS)
    unit = proj * inv
    unit_b = unit.astype(BF16)

    over_y = jnp.concatenate(ring_gather(unit_b[:part_a], "y"), 0)
    over_z = jnp.concatenate(ring_gather(unit_b[part_a:], "z"), 0)
    over_y, over_z = lax.optimization_barrier((over_y, over_z))
    units_a = ring_gather(over_y, "z")
    units_b = ring_gather(over_z, "y")
    grad_unit, grad_proj = pair_grads(
        lists, unit_b, row_ids[:, None], ids, units_a, units_b, unit, inv
    )

    grad_all = gather_dp(grad_proj)
    rows_in = (((0,), (0,)), ((), ()))
    second = lax.dot_general(grad_all, hidden, rows_in, preferred_element_type=F32)
    grad_hidden = lax.dot_general(
        grad_all, w_second, (((1,), (1,)), ((), ())), preferred_element_type=F32
    )
    grad_pre = lax.optimization_barrier((grad_hidden * slope).astype(BF16))
    first = lax.dot_general(rows, grad_pre, rows_in, preferred_element_type=F32)

    def to_y(value):
        return value.reshape(n_z, n_y, -1, share)

    second = to_y(second).swapaxes(0, 1)
    second = lax.psum_scatter(second, "y", scatter_dimension=0, tiled=True)[0]
    second = lax.psum_scatter(second, "z", scatter_dimension=0, tiled=True)[0]

    first = to_y(first)
    first = ring_scatter(
        lambda t: lax.dynamic_index_in_dim(first, lax.rem(y + t + n_y, n_y), 1, False), "y", F32
    )
    first = jnp.sum(lax.all_to_all(first, "z", split_axis=0, concat_axis=0, tiled=True), axis=0)
    return (first, second.T, grad_unit)


def solution(mesh):
    split = Mesh(mesh.devices.reshape(4, 2, 8, 4), ("x", "core", "z", "y"))
    dp, group = ("x", "core"), ("z", "y")
    in_specs = (P(dp + group, None), P(dp + group), P(dp, None), P(None, dp), P(dp, None))
    out_specs = (P(group, dp), P(dp, group), P(dp + group, None))
    return jax.shard_map(
        per_device, mesh=split, in_specs=in_specs, out_specs=out_specs, check_vma=False
    )
```

```python
import jax
import jax.numpy as jnp
from jax import lax
from jax.experimental import pallas as pl
from jax.experimental.pallas import tpu as pltpu
from jax.sharding import Mesh, PartitionSpec as P

EPS = 1e-06
TEMP = 10.0
SHIFT = -5.0
F32, BF16 = jnp.float32, jnp.bfloat16


def gelu_fwd(value):
    return jax.nn.gelu(value, approximate=True)


def gelu_back(pre, grad):
    _, back = jax.vjp(gelu_fwd, pre)
    return back(grad)[0]


def shift(value, axis, step):
    n = lax.axis_size(axis)
    return lax.ppermute(value, axis, [(i, (i + step) % n) for i in range(n)])


def swap_core(value):
    return lax.ppermute(value, "core", [(0, 1), (1, 0)])


def offsets(n):
    out = [0]
    for t in range(1, n // 2):
        out += [-t, t]
    return out + [n // 2]


def slot_of(offset, n):
    table = [0] * n
    for place, t in enumerate(offsets(n)):
        table[t % n] = place
    offset = lax.rem(offset + 2 * n, n)
    return sum(jnp.where(offset == t, table[t], 0) for t in range(1, n))


def ring_gather(block, axis, held=()):
    half, rows = lax.axis_size(axis) // 2, block.shape[0] // 2
    out, up, down = [block], block, block
    for _ in range(1, half):
        up, down = shift(up, axis, 1), shift(down, axis, -1)
        out += [up, down]
    if held:
        *out, held = lax.optimization_barrier((*out, held))
        up, down = out[-2:]
    return out + [shift(up[:rows], axis, 1), shift(down[rows:], axis, -1)], held


def ring_scatter(part, axis, dtype):
    half = lax.axis_size(axis) // 2
    far = part(half)
    rows = far.shape[0] // 2
    up = shift(far[:rows].astype(dtype), axis, 1).astype(F32)
    down = shift(far[rows:].astype(dtype), axis, -1).astype(F32)
    for t in range(half - 1, 0, -1):
        a, b = part(t), part(-t)
        if t == half - 1:
            a = jnp.concatenate([a[:rows] + up, a[rows:]], 0)
            b = jnp.concatenate([b[:rows], b[rows:] + down], 0)
        else:
            a, b = a + up, b + down
        up = shift(a.astype(dtype), axis, 1).astype(F32)
        down = shift(b.astype(dtype), axis, -1).astype(F32)
    return part(0) + up + down


def gather_dp(block):
    (own, up, down, *far), _ = ring_gather(block, "x")
    near, far = jnp.concatenate([up, down], 0), jnp.concatenate(far, 0)
    first = jnp.concatenate([own, near, swap_core(own), swap_core(near)], 0)
    return first, jnp.concatenate([far, swap_core(far)], 0)


def slope_kernel(pre_ref, slope_ref):
    slope_ref[...] = gelu_back(pre_ref[...], jnp.ones(pre_ref.shape, F32))


def gelu_slope(pre):
    spec = pl.BlockSpec((256, pre.shape[1]), lambda i: (i, 0))
    return pl.pallas_call(
        slope_kernel,
        grid=(pre.shape[0] // 256,),
        in_specs=[spec],
        out_specs=spec,
        out_shape=jax.ShapeDtypeStruct(pre.shape, F32),
        cost_estimate=pl.CostEstimate(
            flops=30 * pre.size, bytes_accessed=8 * pre.size, transcendentals=pre.size
        ),
    )(pre)


def pair_kernel(n_z, n_y, copies, at_z, at_y, blocks, mult, count, own_ids_ref, ids_ref,
                proj_ref, *refs):
    n_a, n_b = n_z + 1, n_y + 1
    pieces_a, pieces_b = refs[:n_a], refs[n_a:n_a + n_b]
    grad_unit_ref, grad_proj_ref, own, proj, cand, cand_ids, own_sems, sems = refs[n_a + n_b:]
    block, width = own.shape
    rows_a = pieces_a[0].shape[0] // n_y
    spans = ((0, rows_a), (rows_a, block - rows_a))

    def ids_copy(i, slot, k):
        return pltpu.make_async_copy(
            ids_ref.at[pl.ds(pl.multiple_of(blocks[i] * copies, 8), 8)],
            cand_ids.at[slot, k],
            sems.at[slot, 3 * k + 2],
        )

    def start(pair, slot):
        for k in range(2):
            i = 2 * pair + k
            ids_copy(i, slot, k).start()
            for pieces, outer, inner, n_in, part in (
                (pieces_a, at_z[i], at_y[i], n_y, 0),
                (pieces_b, at_y[i], at_z[i], n_z, 1),
            ):
                far = len(pieces) - 2
                late = (outer == far) & (inner >= n_in // 2)
                source = jnp.where(late, far + 1, outer)
                first, rows = spans[part]
                row = jnp.where(late, inner - n_in // 2, inner) * rows
                for m, piece in enumerate(pieces):

                    @pl.when(source == m)
                    def _():
                        pltpu.make_async_copy(
                            piece.at[pl.ds(pl.multiple_of(row, 16), rows)],
                            cand.at[slot, pl.ds(k * block + first, rows)],
                            sems.at[slot, 3 * k + part],
                        ).start()

    def wait(pair, slot):
        for k in range(2):
            ids_copy(2 * pair + k, slot, k).wait()
            for part, (first, rows) in enumerate(spans):
                pltpu.make_async_copy(
                    pieces_b[0].at[pl.ds(0, rows)],
                    cand.at[slot, pl.ds(k * block + first, rows)],
                    sems.at[slot, 3 * k + part],
                ).wait()

    own_copies = [
        pltpu.make_async_copy(
            piece.at[pl.ds(0, rows)], own.at[pl.ds(first, rows)], own_sems.at[part]
        )
        for part, (piece, (first, rows)) in enumerate(zip((pieces_a[0], pieces_b[0]), spans))
    ]
    proj_copy = pltpu.make_async_copy(proj_ref, proj, own_sems.at[2])
    for copy in own_copies:
        copy.start()
    start(0, 0)
    proj_copy.start()
    grad_unit_ref[...] = jnp.zeros_like(grad_unit_ref)
    for copy in own_copies:
        copy.wait()
    n_pairs = lax.div(count[0] + 1, 2)

    def body(pair, carry):
        slot = lax.rem(pair, 2)

        @pl.when(pair + 1 < n_pairs)
        def _():
            start(pair + 1, 1 - slot)

        wait(pair, slot)
        logits = lax.dot_general(
            own[...], cand[slot], (((1,), (1,)), ((), ())), preferred_element_type=F32
        ) * (TEMP / width) + SHIFT
        ids = jnp.concatenate([cand_ids[slot, 0, :1], cand_ids[slot, 1, :1]], 1)
        sign = jnp.where(own_ids_ref[...] == ids, 1.0, -1.0).astype(F32)
        column = lax.broadcasted_iota(jnp.int32, (1, 2 * block), 1)
        scale = jnp.where(
            column < block, mult[2 * pair].astype(F32), mult[2 * pair + 1].astype(F32)
        ) * (-TEMP / width)
        weight = (sign * scale / (1.0 + jnp.exp(sign * logits))).astype(BF16)
        grad_unit_ref[...] += jnp.dot(weight, cand[slot], preferred_element_type=F32)
        return carry

    lax.fori_loop(0, n_pairs, body, 0)
    proj_copy.wait()
    value, total = proj[...], grad_unit_ref[...]
    inv = lax.rsqrt(jnp.mean(value * value, axis=-1, keepdims=True) + EPS)
    unit = value * inv
    mean = jnp.mean(unit * total, axis=-1, keepdims=True)
    grad_proj_ref[...] = (inv * (total - unit * mean)).astype(BF16)


def pair_grads(lists, own_ids, ids, proj, pieces_a, pieces_b):
    rows, width = proj.shape
    n_z, n_y = len(pieces_a) - 1, len(pieces_b) - 1
    copies = ids.shape[0] // (n_z * n_y)
    vmem = pl.BlockSpec(memory_space=pltpu.VMEM)
    smem = pl.BlockSpec(memory_space=pltpu.SMEM)
    return pl.pallas_call(
        lambda *refs: pair_kernel(n_z, n_y, copies, *refs),
        in_specs=[smem] * 5 + [vmem]
        + [pl.BlockSpec(memory_space=pl.ANY)] * (n_z + n_y + 4),
        out_specs=[vmem] * 2,
        out_shape=[
            jax.ShapeDtypeStruct((rows, width), F32),
            jax.ShapeDtypeStruct((rows, width), BF16),
        ],
        scratch_shapes=[
            pltpu.VMEM((rows, width), BF16),
            pltpu.VMEM((rows, width), F32),
            pltpu.VMEM((2, 2 * rows, width), BF16),
            pltpu.VMEM((2, 2, 8, rows), jnp.int32),
            pltpu.SemaphoreType.DMA((3,)),
            pltpu.SemaphoreType.DMA((2, 6)),
        ],
        compiler_params=pltpu.CompilerParams(vmem_limit_bytes=24 << 20),
    )(*lists, own_ids, ids, proj, *pieces_a, *pieces_b)


def partner_lists(neighbors, n_z, n_y):
    owners = n_z * n_y
    z, y = lax.axis_index("z"), lax.axis_index("y")
    me = z * n_y + y
    block = jnp.arange(owners, dtype=jnp.int32)
    listed = neighbors[None, :, :] == block[:, None, None]
    mine = block == me
    out = jnp.sum(jnp.where(mine[None, :, None], listed, False), axis=(1, 2))
    into = jnp.sum(neighbors == me, axis=1)
    mult = (out + into + 2 * mine).astype(jnp.int32)
    used = mult > 0
    place = jnp.sum(used[None, :] & (block[None, :] < block[:, None]), axis=1)
    pick = used[None, :] & (place[None, :] == block[:, None])
    count = jnp.sum(used).astype(jnp.int32)
    pick = jnp.where((block < count)[:, None], pick, used[None, :] & (place[None, :] == count - 1))
    blocks = jnp.sum(jnp.where(pick, block[None, :], 0), axis=1).astype(jnp.int32)
    mult = jnp.sum(jnp.where(pick, mult[None, :], 0), axis=1)
    mult = jnp.where(block < count, mult, 0).astype(jnp.int32)
    at_z = slot_of(blocks // n_y - z, n_z)
    at_y = slot_of(lax.rem(blocks, n_y) - y, n_y)
    lists = (at_z, at_y, blocks, mult)
    return tuple(v.astype(jnp.int32) for v in lists) + (count[None],)


def per_device(embeds, row_ids, neighbors, w_first, w_second):
    n_z, n_y = lax.axis_size("z"), lax.axis_size("y")
    z, y = lax.axis_index("z"), lax.axis_index("y")
    block, width = embeds.shape[0], w_second.shape[1]
    share = w_first.shape[1]
    part_a = block // 2

    ids, embeds = lax.optimization_barrier((jnp.broadcast_to(row_ids[None], (32, block)), embeds))
    ids = lax.all_gather(ids, "y", axis=0, tiled=True)
    ids = lax.optimization_barrier(lax.all_gather(ids, "z", axis=0, tiled=True))
    lists = partner_lists(neighbors, n_z, n_y)

    rows = gather_dp(embeds)
    pre = [jnp.dot(r, w_first, preferred_element_type=F32) for r in rows]
    hidden = [gelu_fwd(p).astype(BF16) for p in pre]
    hidden = lax.optimization_barrier(hidden)
    parts = [jnp.dot(h, w_second, preferred_element_type=F32).astype(BF16) for h in hidden]
    pair = []
    for part in parts:
        part = part.reshape(2, -1, block, width)
        pair.append(part[0].astype(F32) + swap_core(part[1]).astype(F32))
    term = {0: pair[0][0], -1: pair[0][1], 1: pair[0][2], 2: pair[1][0]}
    proj = ring_scatter(lambda t: term[t], "x", BF16)

    inv = lax.rsqrt(jnp.mean(proj * proj, axis=-1, keepdims=True) + EPS)
    unit_b = (proj * inv).astype(BF16)

    over_y = jnp.concatenate(ring_gather(unit_b[:part_a], "y")[0], 0)
    over_z, (over_y,) = ring_gather(unit_b[part_a:], "z", [over_y])
    over_z = jnp.concatenate(over_z, 0)
    units_a, _ = ring_gather(over_y, "z")
    units_b, (ids, *slope) = ring_gather(over_z, "y", [ids] + [gelu_slope(p) for p in pre])
    grad_unit, grad_proj = pair_grads(
        lists, row_ids[:, None], ids, proj, units_a, units_b
    )

    grads = gather_dp(grad_proj)
    over_rows, over_width = (((0,), (0,)), ((), ())), (((1,), (1,)), ((), ()))

    def product(left, right, over):
        return lax.dot_general(left, right, over, preferred_element_type=F32)

    second = sum(product(g, h, over_rows) for g, h in zip(grads, hidden))
    grad_pre = [(product(g, w_second, over_width) * s).astype(BF16) for g, s in zip(grads, slope)]
    grad_pre = lax.optimization_barrier(grad_pre)
    first = sum(product(r, g, over_rows) for r, g in zip(rows, grad_pre))

    by_zy = first.reshape(n_z, n_y, -1, share)
    first = ring_scatter(
        lambda t: lax.dynamic_index_in_dim(by_zy, lax.rem(y + t + n_y, n_y), 1, False), "y", F32
    )
    first = jnp.sum(lax.all_to_all(first, "z", split_axis=0, concat_axis=0, tiled=True), axis=0)

    second = lax.psum_scatter(second, "z", scatter_dimension=0, tiled=True)
    second, first = lax.optimization_barrier((second, first))
    second = second.reshape(n_y, -1, share)
    second = jnp.sum(lax.all_to_all(second, "y", split_axis=0, concat_axis=0, tiled=True), axis=0)
    return (first, second.T, grad_unit)


def solution(mesh):
    split = Mesh(mesh.devices.reshape(4, 2, 8, 4), ("x", "core", "z", "y"))
    dp, group = ("x", "core"), ("z", "y")
    in_specs = (P(dp + group, None), P(dp + group), P(dp, None), P(None, dp), P(dp, None))
    out_specs = (P(group, dp), P(dp, group), P(dp + group, None))
    return jax.shard_map(
        per_device, mesh=split, in_specs=in_specs, out_specs=out_specs, check_vma=False
    )
```

```python
import jax
import jax.numpy as jnp
from jax import lax
from jax.experimental import pallas as pl
from jax.experimental.pallas import tpu as pltpu
from jax.sharding import Mesh, PartitionSpec as P

EPS = 1e-06
TEMP = 10.0
SHIFT = -5.0
F32, BF16 = jnp.float32, jnp.bfloat16


def gelu_fwd(value):
    return jax.nn.gelu(value, approximate=True)


def gelu_back(pre, grad):
    _, back = jax.vjp(gelu_fwd, pre)
    return back(grad)[0]


def shift(value, axis, step):
    n = lax.axis_size(axis)
    return lax.ppermute(value, axis, [(i, (i + step) % n) for i in range(n)])


def swap_core(value):
    return lax.ppermute(value, "core", [(0, 1), (1, 0)])


def offsets(n):
    out = [0]
    for t in range(1, n // 2):
        out += [-t, t]
    return out + [n // 2]


def slot_of(offset, n):
    table = [0] * n
    for place, t in enumerate(offsets(n)):
        table[t % n] = place
    offset = lax.rem(offset + 2 * n, n)
    return sum(jnp.where(offset == t, table[t], 0) for t in range(1, n))


def ring_gather(block, axis, held=()):
    half, rows = lax.axis_size(axis) // 2, block.shape[0] // 2
    out, up, down = [block], block, block
    for _ in range(1, half):
        up, down = shift(up, axis, 1), shift(down, axis, -1)
        out += [up, down]
    if held:
        *out, held = lax.optimization_barrier((*out, held))
        up, down = out[-2:]
    return out + [shift(up[:rows], axis, 1), shift(down[rows:], axis, -1)], held


def ring_scatter(part, axis, dtype):
    half = lax.axis_size(axis) // 2
    far = part(half)
    rows = far.shape[0] // 2
    up = shift(far[:rows].astype(dtype), axis, 1).astype(F32)
    down = shift(far[rows:].astype(dtype), axis, -1).astype(F32)
    for t in range(half - 1, 0, -1):
        a, b = part(t), part(-t)
        if t == half - 1:
            a = jnp.concatenate([a[:rows] + up, a[rows:]], 0)
            b = jnp.concatenate([b[:rows], b[rows:] + down], 0)
        else:
            a, b = a + up, b + down
        up = shift(a.astype(dtype), axis, 1).astype(F32)
        down = shift(b.astype(dtype), axis, -1).astype(F32)
    return part(0) + up + down


def gather_dp(block, use):
    (own, up, down, *far), _ = ring_gather(block, "x")
    near = jnp.concatenate([up, down], 0)
    first = jnp.concatenate([own, near, swap_core(own), swap_core(near)], 0)
    first = use(first, 0)
    first, far = lax.optimization_barrier((first, far))
    far = jnp.concatenate(far, 0)
    return zip(first, use(jnp.concatenate([far, swap_core(far)], 0), 1))


def slope_kernel(pre_ref, slope_ref):
    slope_ref[...] = gelu_back(pre_ref[...], jnp.ones(pre_ref.shape, F32))


def gelu_slope(pre):
    spec = pl.BlockSpec((256, pre.shape[1]), lambda i: (i, 0))
    return pl.pallas_call(
        slope_kernel,
        grid=(pre.shape[0] // 256,),
        in_specs=[spec],
        out_specs=spec,
        out_shape=jax.ShapeDtypeStruct(pre.shape, F32),
        cost_estimate=pl.CostEstimate(
            flops=30 * pre.size, bytes_accessed=8 * pre.size, transcendentals=pre.size
        ),
    )(pre)


def pair_kernel(n_z, n_y, copies, at_z, at_y, blocks, mult, count, own_ids_ref, ids_ref,
                proj_ref, *refs):
    n_a, n_b = n_z + 1, n_y + 1
    pieces_a, pieces_b = refs[:n_a], refs[n_a:n_a + n_b]
    grad_unit_ref, grad_proj_ref, own, proj, cand, cand_ids, own_sems, sems = refs[n_a + n_b:]
    block, width = own.shape
    rows_a = pieces_a[0].shape[0] // n_y
    spans = ((0, rows_a), (rows_a, block - rows_a))

    def ids_copy(i, slot, k):
        return pltpu.make_async_copy(
            ids_ref.at[pl.ds(pl.multiple_of(blocks[i] * copies, 8), 8)],
            cand_ids.at[slot, k],
            sems.at[slot, 3 * k + 2],
        )

    def start(pair, slot):
        for k in range(2):
            i = 2 * pair + k
            ids_copy(i, slot, k).start()
            for pieces, outer, inner, n_in, part in (
                (pieces_a, at_z[i], at_y[i], n_y, 0),
                (pieces_b, at_y[i], at_z[i], n_z, 1),
            ):
                far = len(pieces) - 2
                late = (outer == far) & (inner >= n_in // 2)
                source = jnp.where(late, far + 1, outer)
                first, rows = spans[part]
                row = jnp.where(late, inner - n_in // 2, inner) * rows
                for m, piece in enumerate(pieces):

                    @pl.when(source == m)
                    def _():
                        pltpu.make_async_copy(
                            piece.at[pl.ds(pl.multiple_of(row, 16), rows)],
                            cand.at[slot, pl.ds(k * block + first, rows)],
                            sems.at[slot, 3 * k + part],
                        ).start()

    def wait(pair, slot):
        for k in range(2):
            ids_copy(2 * pair + k, slot, k).wait()
            for part, (first, rows) in enumerate(spans):
                pltpu.make_async_copy(
                    pieces_b[0].at[pl.ds(0, rows)],
                    cand.at[slot, pl.ds(k * block + first, rows)],
                    sems.at[slot, 3 * k + part],
                ).wait()

    own_copies = [
        pltpu.make_async_copy(
            piece.at[pl.ds(0, rows)], own.at[pl.ds(first, rows)], own_sems.at[part]
        )
        for part, (piece, (first, rows)) in enumerate(zip((pieces_a[0], pieces_b[0]), spans))
    ]
    proj_copy = pltpu.make_async_copy(proj_ref, proj, own_sems.at[2])
    for copy in own_copies:
        copy.start()
    start(0, 0)
    proj_copy.start()
    grad_unit_ref[...] = jnp.zeros_like(grad_unit_ref)
    for copy in own_copies:
        copy.wait()
    n_pairs = lax.div(count[0] + 1, 2)

    def body(pair, carry):
        slot = lax.rem(pair, 2)

        @pl.when(pair + 1 < n_pairs)
        def _():
            start(pair + 1, 1 - slot)

        wait(pair, slot)
        logits = lax.dot_general(
            own[...], cand[slot], (((1,), (1,)), ((), ())), preferred_element_type=F32
        ) * (TEMP / width) + SHIFT
        ids = jnp.concatenate([cand_ids[slot, 0, :1], cand_ids[slot, 1, :1]], 1)
        sign = jnp.where(own_ids_ref[...] == ids, 1.0, -1.0).astype(F32)
        column = lax.broadcasted_iota(jnp.int32, (1, 2 * block), 1)
        scale = jnp.where(
            column < block, mult[2 * pair].astype(F32), mult[2 * pair + 1].astype(F32)
        ) * (-TEMP / width)
        weight = (sign * scale / (1.0 + jnp.exp(sign * logits))).astype(BF16)
        grad_unit_ref[...] += jnp.dot(weight, cand[slot], preferred_element_type=F32)
        return carry

    lax.fori_loop(0, n_pairs, body, 0)
    proj_copy.wait()
    value, total = proj[...], grad_unit_ref[...]
    inv = lax.rsqrt(jnp.mean(value * value, axis=-1, keepdims=True) + EPS)
    unit = value * inv
    mean = jnp.mean(unit * total, axis=-1, keepdims=True)
    grad_proj_ref[...] = (inv * (total - unit * mean)).astype(BF16)


def pair_grads(lists, own_ids, ids, proj, pieces_a, pieces_b):
    rows, width = proj.shape
    n_z, n_y = len(pieces_a) - 1, len(pieces_b) - 1
    copies = ids.shape[0] // (n_z * n_y)
    vmem = pl.BlockSpec(memory_space=pltpu.VMEM)
    smem = pl.BlockSpec(memory_space=pltpu.SMEM)
    return pl.pallas_call(
        lambda *refs: pair_kernel(n_z, n_y, copies, *refs),
        in_specs=[smem] * 5 + [vmem]
        + [pl.BlockSpec(memory_space=pl.ANY)] * (n_z + n_y + 4),
        out_specs=[vmem] * 2,
        out_shape=[
            jax.ShapeDtypeStruct((rows, width), F32),
            jax.ShapeDtypeStruct((rows, width), BF16),
        ],
        scratch_shapes=[
            pltpu.VMEM((rows, width), BF16),
            pltpu.VMEM((rows, width), F32),
            pltpu.VMEM((2, 2 * rows, width), BF16),
            pltpu.VMEM((2, 2, 8, rows), jnp.int32),
            pltpu.SemaphoreType.DMA((3,)),
            pltpu.SemaphoreType.DMA((2, 6)),
        ],
        compiler_params=pltpu.CompilerParams(vmem_limit_bytes=24 << 20),
    )(*lists, own_ids, ids, proj, *pieces_a, *pieces_b)


def partner_lists(neighbors, n_z, n_y):
    owners = n_z * n_y
    z, y = lax.axis_index("z"), lax.axis_index("y")
    me = z * n_y + y
    block = jnp.arange(owners, dtype=jnp.int32)
    listed = neighbors[None, :, :] == block[:, None, None]
    mine = block == me
    out = jnp.sum(jnp.where(mine[None, :, None], listed, False), axis=(1, 2))
    into = jnp.sum(neighbors == me, axis=1)
    mult = (out + into + 2 * mine).astype(jnp.int32)
    used = mult > 0
    place = jnp.sum(used[None, :] & (block[None, :] < block[:, None]), axis=1)
    pick = used[None, :] & (place[None, :] == block[:, None])
    count = jnp.sum(used).astype(jnp.int32)
    pick = jnp.where((block < count)[:, None], pick, used[None, :] & (place[None, :] == count - 1))
    blocks = jnp.sum(jnp.where(pick, block[None, :], 0), axis=1).astype(jnp.int32)
    mult = jnp.sum(jnp.where(pick, mult[None, :], 0), axis=1)
    mult = jnp.where(block < count, mult, 0).astype(jnp.int32)
    at_z = slot_of(blocks // n_y - z, n_z)
    at_y = slot_of(lax.rem(blocks, n_y) - y, n_y)
    lists = (at_z, at_y, blocks, mult)
    return tuple(v.astype(jnp.int32) for v in lists) + (count[None],)


def per_device(embeds, row_ids, neighbors, w_first, w_second):
    n_z, n_y = lax.axis_size("z"), lax.axis_size("y")
    z, y = lax.axis_index("z"), lax.axis_index("y")
    block, width = embeds.shape[0], w_second.shape[1]
    share = w_first.shape[1]
    part_a = block // 2

    ids, embeds = lax.optimization_barrier((jnp.broadcast_to(row_ids[None], (64, block)), embeds))
    ids = lax.all_gather(ids, ("z", "y"), axis=0, tiled=True)
    lists = partner_lists(neighbors, n_z, n_y)

    def forward(rows, _):
        pre = jnp.dot(rows, w_first, preferred_element_type=F32)
        return rows, pre, gelu_fwd(pre).astype(BF16)

    rows, pre, hidden = gather_dp(embeds, forward)
    parts = [jnp.dot(h, w_second, preferred_element_type=F32).astype(BF16) for h in hidden]
    pair = []
    for part in parts:
        part = part.reshape(2, -1, block, width)
        pair.append(part[0].astype(F32) + swap_core(part[1]).astype(F32))
    term = {0: pair[0][0], -1: pair[0][1], 1: pair[0][2], 2: pair[1][0]}
    proj = ring_scatter(lambda t: term[t], "x", BF16)

    inv = lax.rsqrt(jnp.mean(proj * proj, axis=-1, keepdims=True) + EPS)
    unit_b, ids = lax.optimization_barrier(((proj * inv).astype(BF16), ids))

    over_y = jnp.concatenate(ring_gather(unit_b[:part_a], "y")[0], 0)
    over_z, (over_y,) = ring_gather(unit_b[part_a:], "z", [over_y])
    over_z = jnp.concatenate(over_z, 0)
    units_a, _ = ring_gather(over_y, "z")
    units_b, slope = ring_gather(over_z, "y", [gelu_slope(p) for p in pre])
    grad_unit, grad_proj = pair_grads(
        lists, row_ids[:, None], ids, proj, units_a, units_b
    )

    def product(left, right, left_dim, right_dim):
        over = (((left_dim,), (right_dim,)), ((), ()))
        return lax.dot_general(left, right, over, preferred_element_type=F32)

    def backward(grads, k):
        grad_pre = (product(grads, w_second, 1, 1) * slope[k]).astype(BF16)
        grad_pre = lax.optimization_barrier(grad_pre)
        return product(grads, hidden[k], 0, 0), product(rows[k], grad_pre, 0, 0)

    second, first = map(sum, gather_dp(grad_proj, backward))

    by_zy = first.reshape(n_z, n_y, -1, share)
    first = ring_scatter(
        lambda t: lax.dynamic_index_in_dim(by_zy, lax.rem(y + t + n_y, n_y), 1, False), "y", F32
    )
    first = jnp.sum(lax.all_to_all(first, "z", split_axis=0, concat_axis=0, tiled=True), axis=0)

    second = lax.psum_scatter(second, "z", scatter_dimension=0, tiled=True)
    second = second.reshape(n_y, -1, share)
    second = jnp.sum(lax.all_to_all(second, "y", split_axis=0, concat_axis=0, tiled=True), axis=0)
    return (first, second.T, grad_unit)


def solution(mesh):
    split = Mesh(mesh.devices.reshape(4, 2, 8, 4), ("x", "core", "z", "y"))
    dp, group = ("x", "core"), ("z", "y")
    in_specs = (P(dp + group, None), P(dp + group), P(dp, None), P(None, dp), P(dp, None))
    out_specs = (P(group, dp), P(dp, group), P(dp + group, None))
    return jax.shard_map(
        per_device, mesh=split, in_specs=in_specs, out_specs=out_specs, check_vma=False
    )
```

```python
import jax
import jax.numpy as jnp
from jax import lax
from jax.experimental import pallas as pl
from jax.experimental.pallas import tpu as pltpu
from jax.sharding import Mesh, PartitionSpec as P

EPS = 1e-06
TEMP = 10.0
SHIFT = -5.0
F32, BF16 = jnp.float32, jnp.bfloat16
ID_ROWS = 16


def gelu_fwd(value):
    return jax.nn.gelu(value, approximate=True)


def gelu_back(pre, grad):
    _, back = jax.vjp(gelu_fwd, pre)
    return back(grad)[0]


def shift(value, axis, step):
    n = lax.axis_size(axis)
    return lax.ppermute(value, axis, [(i, (i + step) % n) for i in range(n)])


def swap_core(value):
    return lax.ppermute(value, "core", [(0, 1), (1, 0)])


def offsets(n):
    out = [0]
    for t in range(1, n // 2):
        out += [-t, t]
    return out + [n // 2]


def slot_of(offset, n):
    table = [0] * n
    for place, t in enumerate(offsets(n)):
        table[t % n] = place
    offset = lax.rem(offset + 2 * n, n)
    return sum(jnp.where(offset == t, table[t], 0) for t in range(1, n))


def ring_gather(block, axis, *held):
    half, rows = lax.axis_size(axis) // 2, block.shape[0] // 2
    out, up, down = [block], block, block
    for _ in range(1, half):
        up, down = shift(up, axis, 1), shift(down, axis, -1)
        out += [up, down]
    if held:
        out, held = lax.optimization_barrier((out, held))
        up, down = out[-2:]
    return out + [shift(up[:rows], axis, 1), shift(down[rows:], axis, -1), *held]


def ring_scatter(part, axis, dtype):
    half = lax.axis_size(axis) // 2
    far = part(half)
    rows = far.shape[0] // 2
    up = shift(far[:rows].astype(dtype), axis, 1).astype(F32)
    down = shift(far[rows:].astype(dtype), axis, -1).astype(F32)
    for t in range(half - 1, 0, -1):
        a, b = part(t), part(-t)
        if t == half - 1:
            a = jnp.concatenate([a[:rows] + up, a[rows:]], 0)
            b = jnp.concatenate([b[:rows], b[rows:] + down], 0)
        else:
            a, b = a + up, b + down
        up = shift(a.astype(dtype), axis, 1).astype(F32)
        down = shift(b.astype(dtype), axis, -1).astype(F32)
    return part(0) + up + down


def gather_dp(block, use):
    own, up, down, *far = ring_gather(block, "x")
    near = jnp.concatenate([up, down], 0)
    first = jnp.concatenate([own, near, swap_core(own), swap_core(near)], 0)
    first = use(first, 0)
    first, far = lax.optimization_barrier((first, far))
    far = jnp.concatenate(far, 0)
    return zip(first, use(jnp.concatenate([far, swap_core(far)], 0), 1))


def slope_kernel(pre_ref, slope_ref):
    slope_ref[...] = gelu_back(pre_ref[...], jnp.ones(pre_ref.shape, F32))


def gelu_slope(pre):
    spec = pl.BlockSpec((256, pre.shape[1]), lambda i: (i, 0))
    return pl.pallas_call(
        slope_kernel,
        grid=(pre.shape[0] // 256,),
        in_specs=[spec],
        out_specs=spec,
        out_shape=jax.ShapeDtypeStruct(pre.shape, F32),
        cost_estimate=pl.CostEstimate(
            flops=30 * pre.size, bytes_accessed=8 * pre.size, transcendentals=pre.size
        ),
    )(pre)


def pair_kernel(n_z, n_y, groups, at_z, at_y, abs_y, mult, count, own_ids_ref, own_ref,
                proj_ref, *refs):
    pieces = []
    for n_groups, n_out in zip(groups, (n_z, n_y)):
        pieces.append([refs[k * (n_out + 1):][:n_out + 1] for k in range(n_groups)])
        refs = refs[n_groups * (n_out + 1):]
    grad_unit_ref, grad_proj_ref, own, proj, cand, cand_ids, own_sems, sems = refs
    block, width = own.shape
    lengths = pieces[0][0][0].shape[0] * groups[0] // n_y, pieces[1][0][0].shape[0] * groups[1] // n_z
    rows_a = block - lengths[1]
    spans = ((0, rows_a), (rows_a, lengths[1]))

    def ids_copy(piece, row, slot, k):
        return pltpu.make_async_copy(
            piece.at[pl.ds(row, ID_ROWS), pl.ds(0, block)],
            cand_ids.at[slot, k],
            sems.at[slot, 4 + k],
        )

    def start(pair, slot):
        for k in range(2):
            i = 2 * pair + k
            for part, (outer, inner, n_in) in enumerate(
                ((at_z[i], abs_y[i], n_y), (at_y[i], at_z[i], n_z))
            ):
                first, rows = spans[part]
                run = n_in // groups[part]
                for g, group in enumerate(pieces[part]):
                    far = len(group) - 2
                    at = inner - g * run
                    late = (outer == far) & (at >= run // 2)
                    source = jnp.where((at >= 0) & (at < run), jnp.where(late, far + 1, outer), -1)
                    row = jnp.where(late, at - run // 2, at) * lengths[part]
                    row = pl.multiple_of(row, 16)
                    for m, piece in enumerate(group):

                        @pl.when(source == m)
                        def _():
                            pltpu.make_async_copy(
                                piece.at[pl.ds(row, rows)],
                                cand.at[slot, pl.ds(k * block + first, rows)],
                                sems.at[slot, 2 * k + part],
                            ).start()
                            if part == 0:
                                ids_copy(piece, pl.multiple_of(row + rows, 16), slot, k).start()

    def wait(slot):
        for k in range(2):
            ids_copy(pieces[0][0][0], 0, slot, k).wait()
            for part, (first, rows) in enumerate(spans):
                pltpu.make_async_copy(
                    pieces[1][0][0].at[pl.ds(0, rows)],
                    cand.at[slot, pl.ds(k * block + first, rows)],
                    sems.at[slot, 2 * k + part],
                ).wait()

    own_copy = pltpu.make_async_copy(own_ref, own, own_sems.at[0])
    proj_copy = pltpu.make_async_copy(proj_ref, proj, own_sems.at[1])
    own_copy.start()
    start(0, 0)
    proj_copy.start()
    grad_unit_ref[...] = jnp.zeros_like(grad_unit_ref)
    own_copy.wait()
    n_pairs = lax.div(count[0] + 1, 2)

    def body(pair, carry):
        slot = lax.rem(pair, 2)

        @pl.when(pair + 1 < n_pairs)
        def _():
            start(pair + 1, 1 - slot)

        wait(slot)
        logits = lax.dot_general(
            own[...], cand[slot], (((1,), (1,)), ((), ())), preferred_element_type=F32
        ) * (TEMP / width) + SHIFT
        ids = jnp.concatenate([cand_ids[slot, k].astype(F32)[:1] for k in range(2)], 1)
        sign = jnp.where(own_ids_ref[...] == ids, 1.0, -1.0).astype(F32)
        column = lax.broadcasted_iota(jnp.int32, (1, 2 * block), 1)
        scale = jnp.where(
            column < block, mult[2 * pair].astype(F32), mult[2 * pair + 1].astype(F32)
        ) * (-TEMP / width)
        weight = (sign * scale / (1.0 + jnp.exp(sign * logits))).astype(BF16)
        grad_unit_ref[...] += jnp.dot(weight, cand[slot], preferred_element_type=F32)
        return carry

    lax.fori_loop(0, n_pairs, body, 0)
    proj_copy.wait()
    value, total = proj[...], grad_unit_ref[...]
    inv = lax.rsqrt(jnp.mean(value * value, axis=-1, keepdims=True) + EPS)
    unit = value * inv
    mean = jnp.mean(unit * total, axis=-1, keepdims=True)
    grad_proj_ref[...] = (inv * (total - unit * mean)).astype(BF16)


def pair_grads(lists, own_ids, own, proj, units_a, units_b):
    rows, width = proj.shape
    n_z, n_y = len(units_a[0]) - 1, len(units_b[0]) - 1
    groups = len(units_a), len(units_b)
    pieces = sum(units_a + units_b, [])
    vmem = pl.BlockSpec(memory_space=pltpu.VMEM)
    smem = pl.BlockSpec(memory_space=pltpu.SMEM)
    return pl.pallas_call(
        lambda *refs: pair_kernel(n_z, n_y, groups, *refs),
        in_specs=[smem] * 5 + [vmem]
        + [pl.BlockSpec(memory_space=pl.ANY)] * (2 + len(pieces)),
        out_specs=[vmem] * 2,
        out_shape=[
            jax.ShapeDtypeStruct((rows, width), F32),
            jax.ShapeDtypeStruct((rows, width), BF16),
        ],
        scratch_shapes=[
            pltpu.VMEM((rows, width), BF16),
            pltpu.VMEM((rows, width), F32),
            pltpu.VMEM((2, 2 * rows, width), BF16),
            pltpu.VMEM((2, 2, ID_ROWS, rows), BF16),
            pltpu.SemaphoreType.DMA((2,)),
            pltpu.SemaphoreType.DMA((2, 6)),
        ],
        compiler_params=pltpu.CompilerParams(vmem_limit_bytes=48 << 20),
    )(*lists, own_ids, own, proj, *pieces)


def partner_lists(neighbors, n_z, n_y):
    owners = n_z * n_y
    z, y = lax.axis_index("z"), lax.axis_index("y")
    me = z * n_y + y
    block = jnp.arange(owners, dtype=jnp.int32)
    listed = neighbors[None, :, :] == block[:, None, None]
    mine = block == me
    out = jnp.sum(jnp.where(mine[None, :, None], listed, False), axis=(1, 2))
    into = jnp.sum(neighbors == me, axis=1)
    mult = (out + into + 2 * mine).astype(jnp.int32)
    used = mult > 0
    place = jnp.sum(used[None, :] & (block[None, :] < block[:, None]), axis=1)
    pick = used[None, :] & (place[None, :] == block[:, None])
    count = jnp.sum(used).astype(jnp.int32)
    pick = jnp.where((block < count)[:, None], pick, used[None, :] & (place[None, :] == count - 1))
    blocks = jnp.sum(jnp.where(pick, block[None, :], 0), axis=1).astype(jnp.int32)
    mult = jnp.sum(jnp.where(pick, mult[None, :], 0), axis=1)
    mult = jnp.where(block < count, mult, 0).astype(jnp.int32)
    at_z = slot_of(blocks // n_y - z, n_z)
    at_y = slot_of(lax.rem(blocks, n_y) - y, n_y)
    lists = (at_z, at_y, lax.rem(blocks, n_y), mult)
    return tuple(v.astype(jnp.int32) for v in lists) + (count[None],)


def per_device(embeds, row_ids, neighbors, w_first, w_second):
    n_z, n_y = lax.axis_size("z"), lax.axis_size("y")
    z, y = lax.axis_index("z"), lax.axis_index("y")
    block, width = embeds.shape[0], w_second.shape[1]
    share = w_first.shape[1]
    part_a = block * 7 // 16

    lists = partner_lists(neighbors, n_z, n_y)

    def forward(rows, _):
        pre = jnp.dot(rows, w_first, preferred_element_type=F32)
        return rows, pre, gelu_fwd(pre).astype(BF16)

    rows, pre, hidden = gather_dp(embeds, forward)
    parts = [jnp.dot(h, w_second, preferred_element_type=F32).astype(BF16) for h in hidden]
    pair = []
    for part in parts:
        part = part.reshape(2, -1, block, width)
        pair.append(part[0].astype(F32) + swap_core(part[1]).astype(F32))
    term = {0: pair[0][0], -1: pair[0][1], 1: pair[0][2], 2: pair[1][0]}
    proj = ring_scatter(lambda t: term[t], "x", BF16)

    inv = lax.rsqrt(jnp.mean(proj * proj, axis=-1, keepdims=True) + EPS)
    unit_b = (proj * inv).astype(BF16)

    ids = jnp.pad(row_ids.astype(BF16)[None], ((0, ID_ROWS - 1), (0, width - block)))
    over_y = lax.all_gather(jnp.concatenate([unit_b[:part_a], ids], 0), "y", axis=0, tiled=True)
    over_z = jnp.concatenate(ring_gather(unit_b[part_a:], "z"), 0)
    over_y, over_z = lax.optimization_barrier((over_y, over_z))
    units_a = [ring_gather(over_y, "z")]
    *units_b, slope = ring_gather(over_z, "y", [gelu_slope(p) for p in pre])
    units_b = [units_b]
    grad_unit, grad_proj = pair_grads(
        lists, row_ids.astype(F32)[:, None], unit_b, proj, units_a, units_b
    )

    def product(left, right, left_dim, right_dim):
        over = (((left_dim,), (right_dim,)), ((), ()))
        return lax.dot_general(left, right, over, preferred_element_type=F32)

    def backward(grads, k):
        grad_pre = (product(grads, w_second, 1, 1) * slope[k]).astype(BF16)
        grad_pre = lax.optimization_barrier(grad_pre)
        return product(grads, hidden[k], 0, 0), product(rows[k], grad_pre, 0, 0)

    second, first = map(sum, gather_dp(grad_proj, backward))

    by_zy = first.reshape(n_z, n_y, -1, share)
    first = ring_scatter(
        lambda t: lax.dynamic_index_in_dim(by_zy, lax.rem(y + t + n_y, n_y), 1, False), "y", F32
    )
    second = lax.psum_scatter(second, "z", scatter_dimension=0, tiled=True)
    second = second.reshape(n_y, -1, share)
    first = lax.all_to_all(first, "z", split_axis=0, concat_axis=0, tiled=True)
    second = lax.all_to_all(second, "y", split_axis=0, concat_axis=0, tiled=True)
    first, second = lax.optimization_barrier((first, second))
    first, second = jnp.sum(first, axis=0), jnp.sum(second, axis=0)
    return (first, second.T, grad_unit)


def solution(mesh):
    split = Mesh(mesh.devices.reshape(4, 2, 8, 4), ("x", "core", "z", "y"))
    dp, group = ("x", "core"), ("z", "y")
    in_specs = (P(dp + group, None), P(dp + group), P(dp, None), P(None, dp), P(dp, None))
    out_specs = (P(group, dp), P(dp, group), P(dp + group, None))
    return jax.shard_map(
        per_device, mesh=split, in_specs=in_specs, out_specs=out_specs, check_vma=False
    )
```

```python
import jax
import jax.numpy as jnp
from jax import lax
from jax.experimental import pallas as pl
from jax.experimental.pallas import tpu as pltpu
from jax.sharding import Mesh, PartitionSpec as P

EPS = 1e-06
TEMP = 10.0
SHIFT = -5.0
F32, BF16 = jnp.float32, jnp.bfloat16
ID_ROWS = 16


def gelu_fwd(value):
    return jax.nn.gelu(value, approximate=True)


def gelu_back(pre, grad):
    _, back = jax.vjp(gelu_fwd, pre)
    return back(grad)[0]


def shift(value, axis, step):
    n = lax.axis_size(axis)
    return lax.ppermute(value, axis, [(i, (i + step) % n) for i in range(n)])


def swap_core(value):
    return lax.ppermute(value, "core", [(0, 1), (1, 0)])


def offsets(n):
    out = [0]
    for t in range(1, n // 2):
        out += [-t, t]
    return out + [n // 2]


def slot_of(offset, n):
    table = [0] * n
    for place, t in enumerate(offsets(n)):
        table[t % n] = place
    offset = lax.rem(offset + 2 * n, n)
    return sum(jnp.where(offset == t, table[t], 0) for t in range(1, n))


def ring_gather(block, axis, *held):
    half, rows = lax.axis_size(axis) // 2, block.shape[0] // 2
    out, up, down = [block], block, block
    for t in range(1, half):
        up, down = shift(up, axis, 1), shift(down, axis, -1)
        if held and t == 1:
            up, down, held = lax.optimization_barrier((up, down, held))
        out += [up, down]
    return out + [shift(up[:rows], axis, 1), shift(down[rows:], axis, -1), *held]


def ring_scatter(part, axis, dtype):
    half = lax.axis_size(axis) // 2
    far = part(half)
    rows = far.shape[0] // 2
    up = shift(far[:rows].astype(dtype), axis, 1).astype(F32)
    down = shift(far[rows:].astype(dtype), axis, -1).astype(F32)
    for t in range(half - 1, 0, -1):
        a, b = part(t), part(-t)
        if t == half - 1:
            a = jnp.concatenate([a[:rows] + up, a[rows:]], 0)
            b = jnp.concatenate([b[:rows], b[rows:] + down], 0)
        else:
            a, b = a + up, b + down
        up = shift(a.astype(dtype), axis, 1).astype(F32)
        down = shift(b.astype(dtype), axis, -1).astype(F32)
    return part(0) + up + down


def gather_dp(block, use):
    own, up, down, *far = ring_gather(block, "x")
    near = jnp.concatenate([up, down], 0)
    first = jnp.concatenate([own, near, swap_core(own), swap_core(near)], 0)
    first = use(first, 0)
    first, far = lax.optimization_barrier((first, far))
    far = jnp.concatenate(far, 0)
    return zip(first, use(jnp.concatenate([far, swap_core(far)], 0), 1))


def slope_kernel(pre_ref, slope_ref):
    slope_ref[...] = gelu_back(pre_ref[...], jnp.ones(pre_ref.shape, F32))


def gelu_slope(pre):
    spec = pl.BlockSpec((256, pre.shape[1]), lambda i: (i, 0))
    return pl.pallas_call(
        slope_kernel,
        grid=(pre.shape[0] // 256,),
        in_specs=[spec],
        out_specs=spec,
        out_shape=jax.ShapeDtypeStruct(pre.shape, F32),
        cost_estimate=pl.CostEstimate(
            flops=30 * pre.size, bytes_accessed=8 * pre.size, transcendentals=pre.size
        ),
    )(pre)


def pair_kernel(n_z, n_y, groups, at_z, at_y, abs_y, mult, count, own_ids_ref, own_ref,
                proj_ref, *refs):
    pieces = []
    for n_groups, n_out in zip(groups, (n_z, n_y)):
        pieces.append([refs[k * (n_out + 1):][:n_out + 1] for k in range(n_groups)])
        refs = refs[n_groups * (n_out + 1):]
    grad_unit_ref, grad_proj_ref, own, proj, cand, cand_ids, own_sems, sems = refs
    block, width = own.shape
    lengths = pieces[0][0][0].shape[0] * groups[0] // n_y, pieces[1][0][0].shape[0] * groups[1] // n_z
    rows_a = block - lengths[1]
    spans = ((0, rows_a), (rows_a, lengths[1]))

    def ids_copy(piece, row, slot, k):
        return pltpu.make_async_copy(
            piece.at[pl.ds(row, ID_ROWS), pl.ds(0, block)],
            cand_ids.at[slot, k],
            sems.at[slot, 4 + k],
        )

    def start(pair, slot):
        for k in range(2):
            i = 2 * pair + k
            for part, (outer, inner, n_in) in enumerate(
                ((at_z[i], abs_y[i], n_y), (at_y[i], at_z[i], n_z))
            ):
                first, rows = spans[part]
                run = n_in // groups[part]
                for g, group in enumerate(pieces[part]):
                    far = len(group) - 2
                    at = inner - g * run
                    late = (outer == far) & (at >= run // 2)
                    source = jnp.where((at >= 0) & (at < run), jnp.where(late, far + 1, outer), -1)
                    row = jnp.where(late, at - run // 2, at) * lengths[part]
                    row = pl.multiple_of(row, 16)
                    for m, piece in enumerate(group):

                        @pl.when(source == m)
                        def _():
                            pltpu.make_async_copy(
                                piece.at[pl.ds(row, rows)],
                                cand.at[slot, pl.ds(k * block + first, rows)],
                                sems.at[slot, 2 * k + part],
                            ).start()
                            if part == 0:
                                ids_copy(piece, pl.multiple_of(row + rows, 16), slot, k).start()

    def wait(slot):
        for k in range(2):
            ids_copy(pieces[0][0][0], 0, slot, k).wait()
            for part, (first, rows) in enumerate(spans):
                pltpu.make_async_copy(
                    pieces[1][0][0].at[pl.ds(0, rows)],
                    cand.at[slot, pl.ds(k * block + first, rows)],
                    sems.at[slot, 2 * k + part],
                ).wait()

    own_copy = pltpu.make_async_copy(own_ref, own, own_sems.at[0])
    proj_copy = pltpu.make_async_copy(proj_ref, proj, own_sems.at[1])
    own_copy.start()
    start(0, 0)
    proj_copy.start()
    grad_unit_ref[...] = jnp.zeros_like(grad_unit_ref)
    own_copy.wait()
    n_pairs = lax.div(count[0] + 1, 2)

    def body(pair, carry):
        slot = lax.rem(pair, 2)

        @pl.when(pair + 1 < n_pairs)
        def _():
            start(pair + 1, 1 - slot)

        wait(slot)
        logits = lax.dot_general(
            own[...], cand[slot], (((1,), (1,)), ((), ())), preferred_element_type=F32
        ) * (TEMP / width) + SHIFT
        ids = jnp.concatenate([cand_ids[slot, k].astype(F32)[:1] for k in range(2)], 1)
        sign = jnp.where(own_ids_ref[...] == ids, 1.0, -1.0).astype(F32)
        column = lax.broadcasted_iota(jnp.int32, (1, 2 * block), 1)
        scale = jnp.where(
            column < block, mult[2 * pair].astype(F32), mult[2 * pair + 1].astype(F32)
        ) * (-TEMP / width)
        weight = (sign * scale / (1.0 + jnp.exp(sign * logits))).astype(BF16)
        grad_unit_ref[...] += jnp.dot(weight, cand[slot], preferred_element_type=F32)
        return carry

    lax.fori_loop(0, n_pairs, body, 0)
    proj_copy.wait()
    value, total = proj[...], grad_unit_ref[...]
    inv = lax.rsqrt(jnp.mean(value * value, axis=-1, keepdims=True) + EPS)
    unit = value * inv
    mean = jnp.mean(unit * total, axis=-1, keepdims=True)
    grad_proj_ref[...] = (inv * (total - unit * mean)).astype(BF16)


def pair_grads(lists, own_ids, own, proj, units_a, units_b):
    rows, width = proj.shape
    n_z, n_y = len(units_a[0]) - 1, len(units_b[0]) - 1
    groups = len(units_a), len(units_b)
    pieces = sum(units_a + units_b, [])
    vmem = pl.BlockSpec(memory_space=pltpu.VMEM)
    smem = pl.BlockSpec(memory_space=pltpu.SMEM)
    return pl.pallas_call(
        lambda *refs: pair_kernel(n_z, n_y, groups, *refs),
        in_specs=[smem] * 5 + [vmem]
        + [pl.BlockSpec(memory_space=pl.ANY)] * (2 + len(pieces)),
        out_specs=[vmem] * 2,
        out_shape=[
            jax.ShapeDtypeStruct((rows, width), F32),
            jax.ShapeDtypeStruct((rows, width), BF16),
        ],
        scratch_shapes=[
            pltpu.VMEM((rows, width), BF16),
            pltpu.VMEM((rows, width), F32),
            pltpu.VMEM((2, 2 * rows, width), BF16),
            pltpu.VMEM((2, 2, ID_ROWS, rows), BF16),
            pltpu.SemaphoreType.DMA((2,)),
            pltpu.SemaphoreType.DMA((2, 6)),
        ],
        compiler_params=pltpu.CompilerParams(vmem_limit_bytes=48 << 20),
    )(*lists, own_ids, own, proj, *pieces)


def partner_lists(neighbors, n_z, n_y):
    owners = n_z * n_y
    z, y = lax.axis_index("z"), lax.axis_index("y")
    me = z * n_y + y
    block = jnp.arange(owners, dtype=jnp.int32)
    listed = neighbors[None, :, :] == block[:, None, None]
    mine = block == me
    out = jnp.sum(jnp.where(mine[None, :, None], listed, False), axis=(1, 2))
    into = jnp.sum(neighbors == me, axis=1)
    mult = (out + into + 2 * mine).astype(jnp.int32)
    used = mult > 0
    place = jnp.sum(used[None, :] & (block[None, :] < block[:, None]), axis=1)
    pick = used[None, :] & (place[None, :] == block[:, None])
    count = jnp.sum(used).astype(jnp.int32)
    pick = jnp.where((block < count)[:, None], pick, used[None, :] & (place[None, :] == count - 1))
    blocks = jnp.sum(jnp.where(pick, block[None, :], 0), axis=1).astype(jnp.int32)
    mult = jnp.sum(jnp.where(pick, mult[None, :], 0), axis=1)
    mult = jnp.where(block < count, mult, 0).astype(jnp.int32)
    at_z = slot_of(blocks // n_y - z, n_z)
    at_y = slot_of(lax.rem(blocks, n_y) - y, n_y)
    lists = (at_z, at_y, lax.rem(blocks, n_y), mult)
    return tuple(v.astype(jnp.int32) for v in lists) + (count[None],)


def per_device(embeds, row_ids, neighbors, w_first, w_second):
    n_z, n_y = lax.axis_size("z"), lax.axis_size("y")
    z, y = lax.axis_index("z"), lax.axis_index("y")
    block, width = embeds.shape[0], w_second.shape[1]
    share = w_first.shape[1]
    part_a = block * 7 // 16

    lists = partner_lists(neighbors, n_z, n_y)

    def forward(rows, _):
        pre = jnp.dot(rows, w_first, preferred_element_type=F32)
        return rows, pre, gelu_fwd(pre).astype(BF16)

    rows, pre, hidden = gather_dp(embeds, forward)
    parts = [jnp.dot(h, w_second, preferred_element_type=F32).astype(BF16) for h in hidden]
    pair = []
    for part in parts:
        part = part.reshape(2, -1, block, width)
        pair.append(part[0].astype(F32) + swap_core(part[1]).astype(F32))
    term = {0: pair[0][0], -1: pair[0][1], 1: pair[0][2], 2: pair[1][0]}
    proj = ring_scatter(lambda t: term[t], "x", BF16)

    inv = lax.rsqrt(jnp.mean(proj * proj, axis=-1, keepdims=True) + EPS)
    unit_b = (proj * inv).astype(BF16)

    ids = jnp.pad(row_ids.astype(BF16)[None], ((0, ID_ROWS - 1), (0, width - block)))
    over_y = lax.all_gather(jnp.concatenate([unit_b[:part_a], ids], 0), "y", axis=0, tiled=True)
    over_z = jnp.concatenate(ring_gather(unit_b[part_a:], "z"), 0)
    over_y, over_z = lax.optimization_barrier((over_y, over_z))
    *units_a, slope = ring_gather(over_y, "z", [gelu_slope(p) for p in pre])
    units_a, units_b = [units_a], [ring_gather(over_z, "y")]
    grad_unit, grad_proj = pair_grads(
        lists, row_ids.astype(F32)[:, None], unit_b, proj, units_a, units_b
    )

    def product(left, right, left_dim, right_dim):
        over = (((left_dim,), (right_dim,)), ((), ()))
        return lax.dot_general(left, right, over, preferred_element_type=F32)

    def backward(grads, k):
        grad_pre = (product(grads, w_second, 1, 1) * slope[k]).astype(BF16)
        grad_pre = lax.optimization_barrier(grad_pre)
        return product(grads, hidden[k], 0, 0), product(rows[k], grad_pre, 0, 0)

    second, first = map(sum, gather_dp(grad_proj, backward))

    by_zy = first.reshape(n_z, n_y, -1, share)
    first = ring_scatter(
        lambda t: lax.dynamic_index_in_dim(by_zy, lax.rem(y + t + n_y, n_y), 1, False), "y", F32
    )
    first = lax.all_to_all(first, "z", split_axis=0, concat_axis=0, tiled=True)
    second = lax.psum_scatter(second, "z", scatter_dimension=0, tiled=True)
    by_y = second.reshape(n_y, -1, share)
    second = ring_scatter(
        lambda t: lax.dynamic_index_in_dim(by_y, lax.rem(y + t + n_y, n_y), 0, False), "y", F32
    )
    first = jnp.sum(first, axis=0)
    return (first, second.T, grad_unit)


def solution(mesh):
    split = Mesh(mesh.devices.reshape(4, 2, 8, 4), ("x", "core", "z", "y"))
    dp, group = ("x", "core"), ("z", "y")
    in_specs = (P(dp + group, None), P(dp + group), P(dp, None), P(None, dp), P(dp, None))
    out_specs = (P(group, dp), P(dp, group), P(dp + group, None))
    return jax.shard_map(
        per_device, mesh=split, in_specs=in_specs, out_specs=out_specs, check_vma=False
    )
```

```python
import jax
import jax.numpy as jnp
from jax import lax
from jax.experimental import pallas as pl
from jax.experimental.pallas import tpu as pltpu
from jax.sharding import Mesh, PartitionSpec as P

EPS = 1e-06
TEMP = 10.0
SHIFT = -5.0
F32, BF16 = jnp.float32, jnp.bfloat16
ID_ROWS = 16


def gelu_fwd(value):
    return jax.nn.gelu(value, approximate=True)


def gelu_back(pre, grad):
    _, back = jax.vjp(gelu_fwd, pre)
    return back(grad)[0]


def shift(value, axis, step):
    n = lax.axis_size(axis)
    return lax.ppermute(value, axis, [(i, (i + step) % n) for i in range(n)])


def swap_core(value):
    return lax.ppermute(value, "core", [(0, 1), (1, 0)])


def offsets(n):
    out = [0]
    for t in range(1, n // 2):
        out += [-t, t]
    return out + [n // 2]


def slot_of(offset, n):
    table = [0] * n
    for place, t in enumerate(offsets(n)):
        table[t % n] = place
    offset = lax.rem(offset + 2 * n, n)
    return sum(jnp.where(offset == t, table[t], 0) for t in range(1, n))


def ring_gather(block, axis, *held):
    half, rows = lax.axis_size(axis) // 2, block.shape[0] // 2
    out, up, down = [block], block, block
    for t in range(1, half):
        up, down = shift(up, axis, 1), shift(down, axis, -1)
        if held and t == 1:
            up, down, held = lax.optimization_barrier((up, down, held))
        out += [up, down]
    return out + [shift(up[:rows], axis, 1), shift(down[rows:], axis, -1), *held]


def ring_scatter(part, axis, dtype):
    half = lax.axis_size(axis) // 2
    far = part(half)
    rows = far.shape[0] // 2
    up = shift(far[:rows].astype(dtype), axis, 1).astype(F32)
    down = shift(far[rows:].astype(dtype), axis, -1).astype(F32)
    for t in range(half - 1, 0, -1):
        a, b = part(t), part(-t)
        if t == half - 1:
            a = jnp.concatenate([a[:rows] + up, a[rows:]], 0)
            b = jnp.concatenate([b[:rows], b[rows:] + down], 0)
        else:
            a, b = a + up, b + down
        up = shift(a.astype(dtype), axis, 1).astype(F32)
        down = shift(b.astype(dtype), axis, -1).astype(F32)
    return part(0) + up + down


def gather_dp(block, use):
    own, up, down, *far = ring_gather(block, "x")
    near = jnp.concatenate([up, down], 0)
    first = jnp.concatenate([own, near, swap_core(own), swap_core(near)], 0)
    first = use(first, 0)
    first, far = lax.optimization_barrier((first, far))
    far = jnp.concatenate(far, 0)
    return zip(first, use(jnp.concatenate([far, swap_core(far)], 0), 1))


def slope_kernel(pre_ref, slope_ref):
    slope_ref[...] = gelu_back(pre_ref[...], jnp.ones(pre_ref.shape, F32))


def gelu_slope(pre):
    spec = pl.BlockSpec((256, pre.shape[1]), lambda i: (i, 0))
    return pl.pallas_call(
        slope_kernel,
        grid=(pre.shape[0] // 256,),
        in_specs=[spec],
        out_specs=spec,
        out_shape=jax.ShapeDtypeStruct(pre.shape, F32),
        cost_estimate=pl.CostEstimate(
            flops=30 * pre.size, bytes_accessed=8 * pre.size, transcendentals=pre.size
        ),
    )(pre)


def pair_kernel(n_z, n_y, groups, at_z, at_y, abs_y, mult, count, own_ids_ref, own_ref,
                proj_ref, *refs):
    pieces = []
    for n_groups, n_out in zip(groups, (n_z, n_y)):
        pieces.append([refs[k * (n_out + 1):][:n_out + 1] for k in range(n_groups)])
        refs = refs[n_groups * (n_out + 1):]
    grad_unit_ref, grad_proj_ref, own, proj, cand, cand_ids, own_sems, sems = refs
    block, width = own.shape
    lengths = pieces[0][0][0].shape[0] * groups[0] // n_y, pieces[1][0][0].shape[0] * groups[1] // n_z
    rows_a = block - lengths[1]
    spans = ((0, rows_a), (rows_a, lengths[1]))

    def ids_copy(piece, row, slot, k):
        return pltpu.make_async_copy(
            piece.at[pl.ds(row, ID_ROWS), pl.ds(0, block)],
            cand_ids.at[slot, k],
            sems.at[slot, 4 + k],
        )

    def start(pair, slot):
        for k in range(2):
            i = 2 * pair + k
            for part, (outer, inner, n_in) in enumerate(
                ((at_z[i], abs_y[i], n_y), (at_y[i], at_z[i], n_z))
            ):
                first, rows = spans[part]
                run = n_in // groups[part]
                for g, group in enumerate(pieces[part]):
                    far = len(group) - 2
                    at = inner - g * run
                    late = (outer == far) & (at >= run // 2)
                    source = jnp.where((at >= 0) & (at < run), jnp.where(late, far + 1, outer), -1)
                    row = jnp.where(late, at - run // 2, at) * lengths[part]
                    row = pl.multiple_of(row, 16)
                    for m, piece in enumerate(group):

                        @pl.when(source == m)
                        def _():
                            pltpu.make_async_copy(
                                piece.at[pl.ds(row, rows)],
                                cand.at[slot, pl.ds(k * block + first, rows)],
                                sems.at[slot, 2 * k + part],
                            ).start()
                            if part == 0:
                                ids_copy(piece, pl.multiple_of(row + rows, 16), slot, k).start()

    def wait(slot):
        for k in range(2):
            ids_copy(pieces[0][0][0], 0, slot, k).wait()
            for part, (first, rows) in enumerate(spans):
                pltpu.make_async_copy(
                    pieces[1][0][0].at[pl.ds(0, rows)],
                    cand.at[slot, pl.ds(k * block + first, rows)],
                    sems.at[slot, 2 * k + part],
                ).wait()

    own_copy = pltpu.make_async_copy(own_ref, own, own_sems.at[0])
    proj_copy = pltpu.make_async_copy(proj_ref, proj, own_sems.at[1])
    own_copy.start()
    start(0, 0)
    proj_copy.start()
    grad_unit_ref[...] = jnp.zeros_like(grad_unit_ref)
    own_copy.wait()
    n_pairs = lax.div(count[0] + 1, 2)

    def body(pair, carry):
        slot = lax.rem(pair, 2)

        @pl.when(pair + 1 < n_pairs)
        def _():
            start(pair + 1, 1 - slot)

        wait(slot)
        logits = lax.dot_general(
            own[...], cand[slot], (((1,), (1,)), ((), ())), preferred_element_type=F32
        ) * (TEMP / width) + SHIFT
        ids = jnp.concatenate([cand_ids[slot, k].astype(F32)[:1] for k in range(2)], 1)
        sign = jnp.where(own_ids_ref[...] == ids, 1.0, -1.0).astype(F32)
        column = lax.broadcasted_iota(jnp.int32, (1, 2 * block), 1)
        scale = jnp.where(
            column < block, mult[2 * pair].astype(F32), mult[2 * pair + 1].astype(F32)
        ) * (-TEMP / width)
        weight = (sign * scale / (1.0 + jnp.exp(sign * logits))).astype(BF16)
        grad_unit_ref[...] += jnp.dot(weight, cand[slot], preferred_element_type=F32)
        return carry

    lax.fori_loop(0, n_pairs, body, 0)
    proj_copy.wait()
    value, total = proj[...], grad_unit_ref[...]
    inv = lax.rsqrt(jnp.mean(value * value, axis=-1, keepdims=True) + EPS)
    unit = value * inv
    mean = jnp.mean(unit * total, axis=-1, keepdims=True)
    grad_proj_ref[...] = (inv * (total - unit * mean)).astype(BF16)


def pair_grads(lists, own_ids, own, proj, units_a, units_b):
    rows, width = proj.shape
    n_z, n_y = len(units_a[0]) - 1, len(units_b[0]) - 1
    groups = len(units_a), len(units_b)
    pieces = sum(units_a + units_b, [])
    vmem = pl.BlockSpec(memory_space=pltpu.VMEM)
    smem = pl.BlockSpec(memory_space=pltpu.SMEM)
    return pl.pallas_call(
        lambda *refs: pair_kernel(n_z, n_y, groups, *refs),
        in_specs=[smem] * 5 + [vmem]
        + [pl.BlockSpec(memory_space=pl.ANY)] * (2 + len(pieces)),
        out_specs=[vmem] * 2,
        out_shape=[
            jax.ShapeDtypeStruct((rows, width), F32),
            jax.ShapeDtypeStruct((rows, width), BF16),
        ],
        scratch_shapes=[
            pltpu.VMEM((rows, width), BF16),
            pltpu.VMEM((rows, width), F32),
            pltpu.VMEM((2, 2 * rows, width), BF16),
            pltpu.VMEM((2, 2, ID_ROWS, rows), BF16),
            pltpu.SemaphoreType.DMA((2,)),
            pltpu.SemaphoreType.DMA((2, 6)),
        ],
        compiler_params=pltpu.CompilerParams(vmem_limit_bytes=48 << 20),
    )(*lists, own_ids, own, proj, *pieces)


def partner_lists(neighbors, n_z, n_y):
    owners = n_z * n_y
    z, y = lax.axis_index("z"), lax.axis_index("y")
    me = z * n_y + y
    block = jnp.arange(owners, dtype=jnp.int32)
    listed = neighbors[None, :, :] == block[:, None, None]
    mine = block == me
    out = jnp.sum(jnp.where(mine[None, :, None], listed, False), axis=(1, 2))
    into = jnp.sum(neighbors == me, axis=1)
    mult = (out + into + 2 * mine).astype(jnp.int32)
    used = mult > 0
    place = jnp.sum(used[None, :] & (block[None, :] < block[:, None]), axis=1)
    pick = used[None, :] & (place[None, :] == block[:, None])
    count = jnp.sum(used).astype(jnp.int32)
    pick = jnp.where((block < count)[:, None], pick, used[None, :] & (place[None, :] == count - 1))
    blocks = jnp.sum(jnp.where(pick, block[None, :], 0), axis=1).astype(jnp.int32)
    mult = jnp.sum(jnp.where(pick, mult[None, :], 0), axis=1)
    mult = jnp.where(block < count, mult, 0).astype(jnp.int32)
    at_z = slot_of(blocks // n_y - z, n_z)
    at_y = slot_of(lax.rem(blocks, n_y) - y, n_y)
    lists = (at_z, at_y, lax.rem(blocks, n_y), mult)
    return tuple(v.astype(jnp.int32) for v in lists) + (count[None],)


def per_device(embeds, row_ids, neighbors, w_first, w_second):
    n_z, n_y = lax.axis_size("z"), lax.axis_size("y")
    z, y = lax.axis_index("z"), lax.axis_index("y")
    block, width = embeds.shape[0], w_second.shape[1]
    share = w_first.shape[1]
    part_a = block * 7 // 16

    lists = partner_lists(neighbors, n_z, n_y)

    def forward(rows, _):
        pre = jnp.dot(rows, w_first, preferred_element_type=F32)
        return rows, pre, gelu_fwd(pre).astype(BF16)

    rows, pre, hidden = gather_dp(embeds, forward)
    parts = [jnp.dot(h, w_second, preferred_element_type=F32).astype(BF16) for h in hidden]
    pair = []
    for part in parts:
        part = part.reshape(2, -1, block, width)
        pair.append(part[0].astype(F32) + swap_core(part[1]).astype(F32))
    term = {0: pair[0][0], -1: pair[0][1], 1: pair[0][2], 2: pair[1][0]}
    proj = ring_scatter(lambda t: term[t], "x", BF16)

    inv = lax.rsqrt(jnp.mean(proj * proj, axis=-1, keepdims=True) + EPS)
    unit_b = (proj * inv).astype(BF16)

    ids = jnp.pad(row_ids.astype(BF16)[None], ((0, ID_ROWS - 1), (0, width - block)))
    over_y = lax.all_gather(jnp.concatenate([unit_b[:part_a], ids], 0), "y", axis=0, tiled=True)
    over_z = jnp.concatenate(ring_gather(unit_b[part_a:], "z"), 0)
    over_y, over_z = lax.optimization_barrier((over_y, over_z))
    *units_a, slope = ring_gather(over_y, "z", [gelu_slope(p) for p in pre])
    units_a, units_b = [units_a], [ring_gather(over_z, "y")]
    grad_unit, grad_proj = pair_grads(
        lists, row_ids.astype(F32)[:, None], unit_b, proj, units_a, units_b
    )

    def product(left, right, left_dim, right_dim):
        over = (((left_dim,), (right_dim,)), ((), ()))
        return lax.dot_general(left, right, over, preferred_element_type=F32)

    def backward(grads, k):
        grad_pre = (product(grads, w_second, 1, 1) * slope[k]).astype(BF16)
        grad_pre = lax.optimization_barrier(grad_pre)
        return product(grads, hidden[k], 0, 0), product(rows[k], grad_pre, 0, 0)

    second, first = map(sum, gather_dp(grad_proj, backward))

    by_zy = first.reshape(n_z, n_y, -1, share)
    first = ring_scatter(
        lambda t: lax.dynamic_index_in_dim(by_zy, lax.rem(y + t + n_y, n_y), 1, False), "y", F32
    )
    first = lax.all_to_all(first, "z", split_axis=0, concat_axis=0, tiled=True)
    all_second = second.reshape(n_z, n_y, -1, share)
    by_y = ring_scatter(
        lambda t: lax.dynamic_index_in_dim(all_second, lax.rem(z + t + n_z, n_z), 0, False), "z", F32
    )
    second = ring_scatter(
        lambda t: lax.dynamic_index_in_dim(by_y, lax.rem(y + t + n_y, n_y), 0, False), "y", F32
    )
    first = jnp.sum(first, axis=0)
    return (first, second.T, grad_unit)


def solution(mesh):
    split = Mesh(mesh.devices.reshape(4, 2, 8, 4), ("x", "core", "z", "y"))
    dp, group = ("x", "core"), ("z", "y")
    in_specs = (P(dp + group, None), P(dp + group), P(dp, None), P(None, dp), P(dp, None))
    out_specs = (P(group, dp), P(dp, group), P(dp + group, None))
    return jax.shard_map(
        per_device, mesh=split, in_specs=in_specs, out_specs=out_specs, check_vma=False
    )
```

```python
import jax
import jax.numpy as jnp
from jax import lax
from jax.experimental import pallas as pl
from jax.experimental.pallas import tpu as pltpu
from jax.sharding import Mesh, PartitionSpec as P

EPS = 1e-06
TEMP = 10.0
SHIFT = -5.0
F32, BF16 = jnp.float32, jnp.bfloat16
ID_ROWS = 16
LOG2_E = 1.4426950408889634
BLOCKS = 4


def gelu_fwd(value):
    return jax.nn.gelu(value, approximate=True)


def gelu_back(pre, grad):
    _, back = jax.vjp(gelu_fwd, pre)
    return back(grad)[0]


def shift(value, axis, step):
    n = lax.axis_size(axis)
    return lax.ppermute(value, axis, [(i, (i + step) % n) for i in range(n)])


def swap_core(value):
    return lax.ppermute(value, "core", [(0, 1), (1, 0)])


def offsets(n):
    out = [0]
    for t in range(1, n // 2):
        out += [-t, t]
    return out + [n // 2]


def slot_of(offset, n):
    table = [0] * n
    for place, t in enumerate(offsets(n)):
        table[t % n] = place
    offset = lax.rem(offset + 2 * n, n)
    return sum(jnp.where(offset == t, table[t], 0) for t in range(1, n))


def ring_gather(block, axis, *held):
    half, rows = lax.axis_size(axis) // 2, block.shape[0] // 2
    out, up, down = [block], block, block
    for t in range(1, half):
        up, down = shift(up, axis, 1), shift(down, axis, -1)
        if held and t == 1:
            up, down, held = lax.optimization_barrier((up, down, held))
        out += [up, down]
    return out + [shift(up[:rows], axis, 1), shift(down[rows:], axis, -1), *held]


def ring_scatter(part, axis, dtype):
    half = lax.axis_size(axis) // 2
    far = part(half)
    rows = far.shape[0] // 2
    up = shift(far[:rows].astype(dtype), axis, 1).astype(F32)
    down = shift(far[rows:].astype(dtype), axis, -1).astype(F32)
    for t in range(half - 1, 0, -1):
        a, b = part(t), part(-t)
        if t == half - 1:
            a = jnp.concatenate([a[:rows] + up, a[rows:]], 0)
            b = jnp.concatenate([b[:rows], b[rows:] + down], 0)
        else:
            a, b = a + up, b + down
        up = shift(a.astype(dtype), axis, 1).astype(F32)
        down = shift(b.astype(dtype), axis, -1).astype(F32)
    return part(0) + up + down


def gather_dp(block, use):
    own, up, down, *far = ring_gather(block, "x")
    near = jnp.concatenate([up, down], 0)
    first = jnp.concatenate([own, near, swap_core(own), swap_core(near)], 0)
    first = use(first, 0)
    first, far = lax.optimization_barrier((first, far))
    far = jnp.concatenate(far, 0)
    return zip(first, use(jnp.concatenate([far, swap_core(far)], 0), 1))


def slope_kernel(pre_ref, slope_ref):
    slope_ref[...] = gelu_back(pre_ref[...], jnp.ones(pre_ref.shape, F32))


def gelu_slope(pre):
    spec = pl.BlockSpec((256, pre.shape[1]), lambda i: (i, 0))
    return pl.pallas_call(
        slope_kernel,
        grid=(pre.shape[0] // 256,),
        in_specs=[spec],
        out_specs=spec,
        out_shape=jax.ShapeDtypeStruct(pre.shape, F32),
        cost_estimate=pl.CostEstimate(
            flops=30 * pre.size, bytes_accessed=8 * pre.size, transcendentals=pre.size
        ),
    )(pre)


def pair_kernel(n_z, n_y, groups, at_z, at_y, abs_y, mult, count, own_ids_ref, own_ref,
                proj_ref, *refs):
    pieces = []
    for n_groups, n_out in zip(groups, (n_z, n_y)):
        pieces.append([refs[k * (n_out + 1):][:n_out + 1] for k in range(n_groups)])
        refs = refs[n_groups * (n_out + 1):]
    grad_unit_ref, grad_proj_ref, own, proj, cand, cand_ids, own_sems, sems = refs
    block, width = own.shape
    lengths = pieces[0][0][0].shape[0] * groups[0] // n_y, pieces[1][0][0].shape[0] * groups[1] // n_z
    rows_a = block - lengths[1]
    spans = ((0, rows_a), (rows_a, lengths[1]))

    def ids_copy(piece, row, slot, k):
        return pltpu.make_async_copy(
            piece.at[pl.ds(row, ID_ROWS), pl.ds(0, block)],
            cand_ids.at[slot, k],
            sems.at[slot, 3 * k + 2],
        )

    def start(step, slot):
        for k in range(BLOCKS):
            i = BLOCKS * step + k
            for part, (outer, inner, n_in) in enumerate(
                ((at_z[i], abs_y[i], n_y), (at_y[i], at_z[i], n_z))
            ):
                first, rows = spans[part]
                run = n_in // groups[part]
                for g, group in enumerate(pieces[part]):
                    far = len(group) - 2
                    at = inner - g * run
                    late = (outer == far) & (at >= run // 2)
                    source = jnp.where((at >= 0) & (at < run), jnp.where(late, far + 1, outer), -1)
                    row = jnp.where(late, at - run // 2, at) * lengths[part]
                    row = pl.multiple_of(row, 16)
                    for m, piece in enumerate(group):

                        @pl.when(source == m)
                        def _():
                            pltpu.make_async_copy(
                                piece.at[pl.ds(row, rows)],
                                cand.at[slot, pl.ds(k * block + first, rows)],
                                sems.at[slot, 3 * k + part],
                            ).start()
                            if part == 0:
                                ids_copy(piece, pl.multiple_of(row + rows, 16), slot, k).start()

    def wait(slot):
        for k in range(BLOCKS):
            ids_copy(pieces[0][0][0], 0, slot, k).wait()
            for part, (first, rows) in enumerate(spans):
                pltpu.make_async_copy(
                    pieces[1][0][0].at[pl.ds(0, rows)],
                    cand.at[slot, pl.ds(k * block + first, rows)],
                    sems.at[slot, 3 * k + part],
                ).wait()

    own_copy = pltpu.make_async_copy(own_ref, own, own_sems.at[0])
    proj_copy = pltpu.make_async_copy(proj_ref, proj, own_sems.at[1])
    own_copy.start()
    start(0, 0)
    proj_copy.start()
    grad_unit_ref[...] = jnp.zeros_like(grad_unit_ref)
    own_copy.wait()
    n_steps = lax.div(count[0] + BLOCKS - 1, BLOCKS)
    slope, shift_2 = TEMP / width * LOG2_E, SHIFT * LOG2_E
    column = lax.broadcasted_iota(jnp.int32, (1, 2 * block), 1)

    def body(step, carry):
        slot = lax.rem(step, 2)

        @pl.when(step + 1 < n_steps)
        def _():
            start(step + 1, 1 - slot)

        wait(slot)
        weights = []
        for k in range(0, BLOCKS, 2):
            dots = lax.dot_general(
                own[...],
                cand[slot, k * block:(k + 2) * block],
                (((1,), (1,)), ((), ())),
                preferred_element_type=F32,
            )
            ids = jnp.concatenate([cand_ids[slot, k + m].astype(F32)[:1] for m in range(2)], 1)
            same = own_ids_ref[...] == ids
            power = dots * jnp.where(same, slope, -slope) + jnp.where(same, shift_2, -shift_2)
            i = BLOCKS * step + k
            scale = jnp.where(column < block, mult[i].astype(F32), mult[i + 1].astype(F32))
            scale = scale * (TEMP / width)
            weights.append(
                (jnp.where(same, -scale, scale) / (1.0 + jnp.exp2(power))).astype(BF16)
            )
        grad = sum(
            jnp.dot(
                w, cand[slot, 2 * n * block:2 * (n + 1) * block], preferred_element_type=F32
            )
            for n, w in enumerate(weights)
        )
        grad_unit_ref[...] += grad
        return carry

    lax.fori_loop(0, n_steps, body, 0)
    proj_copy.wait()
    value, total = proj[...], grad_unit_ref[...]
    inv = lax.rsqrt(jnp.mean(value * value, axis=-1, keepdims=True) + EPS)
    unit = value * inv
    mean = jnp.mean(unit * total, axis=-1, keepdims=True)
    grad_proj_ref[...] = (inv * (total - unit * mean)).astype(BF16)


def pair_grads(lists, own_ids, own, proj, units_a, units_b):
    rows, width = proj.shape
    n_z, n_y = len(units_a[0]) - 1, len(units_b[0]) - 1
    groups = len(units_a), len(units_b)
    pieces = sum(units_a + units_b, [])
    vmem = pl.BlockSpec(memory_space=pltpu.VMEM)
    smem = pl.BlockSpec(memory_space=pltpu.SMEM)
    return pl.pallas_call(
        lambda *refs: pair_kernel(n_z, n_y, groups, *refs),
        in_specs=[smem] * 5 + [vmem]
        + [pl.BlockSpec(memory_space=pl.ANY)] * (2 + len(pieces)),
        out_specs=[vmem] * 2,
        out_shape=[
            jax.ShapeDtypeStruct((rows, width), F32),
            jax.ShapeDtypeStruct((rows, width), BF16),
        ],
        scratch_shapes=[
            pltpu.VMEM((rows, width), BF16),
            pltpu.VMEM((rows, width), F32),
            pltpu.VMEM((2, BLOCKS * rows, width), BF16),
            pltpu.VMEM((2, BLOCKS, ID_ROWS, rows), BF16),
            pltpu.SemaphoreType.DMA((2,)),
            pltpu.SemaphoreType.DMA((2, 3 * BLOCKS)),
        ],
        compiler_params=pltpu.CompilerParams(vmem_limit_bytes=48 << 20),
    )(*lists, own_ids, own, proj, *pieces)


def partner_lists(neighbors, n_z, n_y):
    owners = n_z * n_y
    z, y = lax.axis_index("z"), lax.axis_index("y")
    me = z * n_y + y
    block = jnp.arange(owners, dtype=jnp.int32)
    listed = neighbors[None, :, :] == block[:, None, None]
    mine = block == me
    out = jnp.sum(jnp.where(mine[None, :, None], listed, False), axis=(1, 2))
    into = jnp.sum(neighbors == me, axis=1)
    mult = (out + into + 2 * mine).astype(jnp.int32)
    used = mult > 0
    place = jnp.sum(used[None, :] & (block[None, :] < block[:, None]), axis=1)
    pick = used[None, :] & (place[None, :] == block[:, None])
    count = jnp.sum(used).astype(jnp.int32)
    pick = jnp.where((block < count)[:, None], pick, used[None, :] & (place[None, :] == count - 1))
    blocks = jnp.sum(jnp.where(pick, block[None, :], 0), axis=1).astype(jnp.int32)
    mult = jnp.sum(jnp.where(pick, mult[None, :], 0), axis=1)
    mult = jnp.where(block < count, mult, 0).astype(jnp.int32)
    at_z = slot_of(blocks // n_y - z, n_z)
    at_y = slot_of(lax.rem(blocks, n_y) - y, n_y)
    lists = (at_z, at_y, lax.rem(blocks, n_y), mult)
    return tuple(v.astype(jnp.int32) for v in lists) + (count[None],)


def per_device(embeds, row_ids, neighbors, w_first, w_second):
    n_z, n_y = lax.axis_size("z"), lax.axis_size("y")
    z, y = lax.axis_index("z"), lax.axis_index("y")
    block, width = embeds.shape[0], w_second.shape[1]
    share = w_first.shape[1]
    part_a = block * 7 // 16

    lists = partner_lists(neighbors, n_z, n_y)

    def forward(rows, _):
        pre = jnp.dot(rows, w_first, preferred_element_type=F32)
        return rows, pre, gelu_fwd(pre).astype(BF16)

    rows, pre, hidden = gather_dp(embeds, forward)
    parts = [jnp.dot(h, w_second, preferred_element_type=F32).astype(BF16) for h in hidden]
    pair = []
    for part in parts:
        part = part.reshape(2, -1, block, width)
        pair.append(part[0].astype(F32) + swap_core(part[1]).astype(F32))
    term = {0: pair[0][0], -1: pair[0][1], 1: pair[0][2], 2: pair[1][0]}
    proj = ring_scatter(lambda t: term[t], "x", BF16)

    inv = lax.rsqrt(jnp.mean(proj * proj, axis=-1, keepdims=True) + EPS)
    unit_b = (proj * inv).astype(BF16)

    ids = jnp.pad(row_ids.astype(BF16)[None], ((0, ID_ROWS - 1), (0, width - block)))
    over_y = lax.all_gather(jnp.concatenate([unit_b[:part_a], ids], 0), "y", axis=0, tiled=True)
    over_z = jnp.concatenate(ring_gather(unit_b[part_a:], "z"), 0)
    over_y, over_z = lax.optimization_barrier((over_y, over_z))
    *units_a, slope = ring_gather(over_y, "z", [gelu_slope(p) for p in pre])
    units_a, units_b = [units_a], [ring_gather(over_z, "y")]
    grad_unit, grad_proj = pair_grads(
        lists, row_ids.astype(F32)[:, None], unit_b, proj, units_a, units_b
    )

    def product(left, right, left_dim, right_dim):
        over = (((left_dim,), (right_dim,)), ((), ()))
        return lax.dot_general(left, right, over, preferred_element_type=F32)

    def backward(grads, k):
        grad_pre = (product(grads, w_second, 1, 1) * slope[k]).astype(BF16)
        grad_pre = lax.optimization_barrier(grad_pre)
        return product(grads, hidden[k], 0, 0), product(rows[k], grad_pre, 0, 0)

    second, first = map(sum, gather_dp(grad_proj, backward))

    by_zy = first.reshape(n_z, n_y, -1, share)
    first = ring_scatter(
        lambda t: lax.dynamic_index_in_dim(by_zy, lax.rem(y + t + n_y, n_y), 1, False), "y", F32
    )
    first = lax.all_to_all(first, "z", split_axis=0, concat_axis=0, tiled=True)
    second = lax.psum_scatter(second, "z", scatter_dimension=0, tiled=True)
    by_y = second.reshape(n_y, -1, share)
    second = ring_scatter(
        lambda t: lax.dynamic_index_in_dim(by_y, lax.rem(y + t + n_y, n_y), 0, False), "y", F32
    )
    first = jnp.sum(first, axis=0)
    return (first, second.T, grad_unit)


def solution(mesh):
    split = Mesh(mesh.devices.reshape(4, 2, 8, 4), ("x", "core", "z", "y"))
    dp, group = ("x", "core"), ("z", "y")
    in_specs = (P(dp + group, None), P(dp + group), P(dp, None), P(None, dp), P(dp, None))
    out_specs = (P(group, dp), P(dp, group), P(dp + group, None))
    return jax.shard_map(
        per_device, mesh=split, in_specs=in_specs, out_specs=out_specs, check_vma=False
    )
```
